32 devices in a mesh: groups: 2 (over y), work: 4 (over z), pol: 2 (over x), vis: 2 (over core).
Axes of the slice: x: 2, y: 2, z: 4, core: 2. Of those that a mesh axis runs over, the one named last changes fastest.
Arguments:
- facets: bfloat16 [128, 4, 8, 2048], P(('groups', 'work'), 'pol', 'vis'), parts along dimension 0, may hold values from -6 to 6
- subgrid_offset: int32 [16], P('groups'), parts along dimension 0, may hold values from 0 to 65535
- tile_subgrid: int32 [64], P(('groups', 'work', 'vis')), parts along dimension 0, may hold values from 0 to 1
- tile_count: int32 [64], P(('groups', 'work', 'vis')), parts along dimension 0, may hold values from 1 to 1024, as said below
- vis_coord: float32 [64, 2, 1024], P(('groups', 'work', 'vis')), parts along dimension 0, may hold values from 0 to 1
- stations: int32 [32, 2, 1024], P(('work', 'vis')), may hold values from 0 to 511
- jones: float32 [8, 1024], P(None, 'groups'), parts along dimension 1, may hold values from -4 to 4
- observed: float32 [64, 4, 2, 1024], P(('groups', 'work', 'vis'), 'pol'), parts along dimension 0, may hold values from -6 to 6
Outputs:
- residual_vis: float32 [64, 4, 2, 1024], P(('groups', 'work', 'vis'), 'pol'), parts along dimension 0
- residual_image: float32 [128, 4, 8, 2048], P(('groups', 'work'), 'pol', 'vis'), parts along dimension 0
The draws below stay inside these ranges and needn't reach their ends.
There are 2 independent parts, one for each index of `groups`. The reference program is written for one: setup_inputs(seed, part) draws one part's arguments, and reference() takes and returns one part's arrays. A program takes and returns all parts, laid end to end along the dimension named above; an argument that names none is the same for every part. Nothing has to cross between parts.
Inputs may be any that keep to these rules, and one draw needn't show every extreme that they name: `tile_subgrid`: blocks are laid out worker by worker, 4 * 2 blocks a worker; each names one of its worker's subgrids. `tile_count`: visibility slots at or beyond the count are padding.
All inputs are finite; a program needn't handle non-finite values.
Results may differ from the reference program's by a relative error of at most 0.025.
Values may be sent and summed in bfloat16 or wider, within the bound.
A program may use at most 128 MiB of HBM per device.

```python
import math
import jax
import jax.numpy as jnp
from jax import lax

FACETS = 64
FS = 1024
SS = 512
ROWS = 8
SG_DEV = 2
TILE = 1024
TILE_DEV = 4
STATIONS = 512
N_IMG = 65536
SUBGRIDS = 8
TILES = 32
N_WORK = 4
N_VIS = 2


def draw_tile_count(key, part):
    first_key, second_key = jax.random.split(jax.random.fold_in(key, 7))
    per_worker = TILE_DEV * N_VIS
    loads = jax.random.randint(first_key, (TILES // per_worker,), 1, 9)
    base = jax.random.randint(second_key, (TILES,), 1, TILE + 1)
    counts = base * jnp.repeat(loads, per_worker) // 4
    counts = jnp.minimum(TILE, jnp.maximum(1, counts))
    counts = counts.at[0].set(TILE)
    return counts.astype(jnp.int32)


def set_ends(values, stream_key, low, largest):
    shape = values.shape
    index_at = [jax.random.randint(jax.random.fold_in(stream_key, axis), (), 0, shape[axis]) for axis in range(len(shape))]
    values = values.at[tuple(index_at)].set(low)
    longest = shape.index(max(shape))
    index_at[longest] = (index_at[longest] + 1) % shape[longest]
    return values.at[tuple(index_at)].set(largest)


def steps_of(key, shape, cuts, least, largest):
    def one(position, shards_of):
        draws = jax.random.uniform(jax.random.fold_in(jax.random.fold_in(key, 6), position), (shards_of,), jnp.float32, least / len(cuts), largest / len(cuts))
        return jnp.repeat(jnp.exp(draws), shape[position] // shards_of).reshape((-1,) + (1,) * (len(shape) - position - 1))

    level = one(*cuts[0])
    for cut in cuts[1:]:
        level = level * one(*cut)
    return level


def normal_values(own_key, extent, width, bound, cuts=(), kind=jnp.bfloat16):
    drawn = jax.random.normal(own_key, extent, jnp.float32) * width
    if len(cuts) > 0:
        drawn = steps_of(own_key, extent, cuts, -0.22, 0.18) * drawn
    return jnp.clip(drawn, min=-bound, max=bound).astype(kind)


def setup_inputs(seed: int = 0, part: int = 0) -> dict:
    key_list = jax.random.split(jax.random.key(seed), 9)
    own_keys = jax.random.split(jax.random.fold_in(key_list[8], part), 9)
    return {
        "facets": normal_values(own_keys[0], (FACETS, 4, ROWS, 2 * FS), 1.0, 6.0, ((0, 4), (1, 2), (2, 2))),
        "subgrid_offset": set_ends(jax.random.randint(own_keys[1], (SUBGRIDS,), 0, N_IMG), jax.random.fold_in(own_keys[1], 1), 0, N_IMG - 1).astype(jnp.int32),
        "tile_subgrid": set_ends(jax.random.randint(own_keys[2], (TILES,), 0, SG_DEV), jax.random.fold_in(own_keys[2], 1), 0, SG_DEV - 1).astype(jnp.int32),
        "tile_count": draw_tile_count(jax.random.fold_in(jax.random.fold_in(key_list[8], part), 71), part),
        "vis_coord": jnp.clip(1.0 * jax.random.uniform(own_keys[4], (TILES, 2, TILE), jnp.float32) ** steps_of(own_keys[4], (TILES, 2, TILE), ((0, 8),), -0.2, 0.2), 0.0, 1.0),
        "stations": set_ends(jax.random.randint(key_list[5], (TILES, 2, TILE), 0, STATIONS), jax.random.fold_in(key_list[5], 1), 0, STATIONS - 1).astype(jnp.int32),
        "jones": normal_values(own_keys[6], (8, STATIONS), 0.6, 4.0, (), jnp.float32),
        "observed": normal_values(own_keys[7], (TILES, 4, 2, TILE), 1.0, 6.0, ((0, 8), (1, 2)), jnp.float32),
    }


TWO_PI = 2.0 * math.pi

def complex_mul(a, b):
    return (a[0] * b[0] - a[1] * b[1], a[0] * b[1] + a[1] * b[0])

def complex_conj(a):
    return (a[0], -a[1])

def complex_add(a, b):
    return (a[0] + b[0], a[1] + b[1])

def jones_matrix(table, pairs, column):
    picked = jnp.take(table, pairs[:, column, :], axis=1)
    return [[(picked[0], picked[4]), (picked[1], picked[5])], [(picked[2], picked[6]), (picked[3], picked[7])]]

def pol_matrix(visible):
    return [[(visible[:, 2 * i + k, 0], visible[:, 2 * i + k, 1]) for k in range(2)] for i in range(2)]

def pack_matrix(matrix):
    return jnp.stack([jnp.stack(matrix[i][k], 1) for i in range(2) for k in range(2)], 1)

def apply_jones(left, right, visible):
    bright = pol_matrix(visible)
    inner = [[complex_add(complex_mul(left[i][0], bright[0][l]), complex_mul(left[i][1], bright[1][l])) for l in range(2)] for i in range(2)]
    outer = [[complex_add(complex_mul(inner[i][0], complex_conj(right[k][0])), complex_mul(inner[i][1], complex_conj(right[k][1]))) for k in range(2)] for i in range(2)]
    return pack_matrix(outer)

def adjoint_jones(left, right, visible):
    resid = pol_matrix(visible)
    inner = [[complex_add(complex_mul(complex_conj(left[0][j]), resid[0][k]), complex_mul(complex_conj(left[1][j]), resid[1][k])) for k in range(2)] for j in range(2)]
    outer = [[complex_add(complex_mul(inner[j][0], right[0][l]), complex_mul(inner[j][1], right[1][l])) for l in range(2)] for j in range(2)]
    return pack_matrix(outer)

def transform_tables():
    image_len = FACETS * FS
    xcells = jnp.arange(FS, dtype=jnp.int32)
    ucells = jnp.arange(SS, dtype=jnp.int32)
    turn = -TWO_PI * (xcells[:, None] * ucells[None, :] % image_len).astype(jnp.float32) / image_len
    cosine = jnp.cos(turn)
    sine_table = jnp.sin(turn)
    forward = jnp.concatenate([jnp.concatenate([cosine, sine_table], 1), jnp.concatenate([-sine_table, cosine], 1)], 0)
    backward = jnp.concatenate([jnp.concatenate([cosine.T, -sine_table.T], 1), jnp.concatenate([sine_table.T, cosine.T], 1)], 0)
    return (forward.astype(jnp.bfloat16), backward.astype(jnp.bfloat16))

def to_subgrids(facet_blk, facet_start, offsets, forward):
    facet_count = facet_blk.shape[0]
    facet_len = facet_blk.shape[-1] // 2
    subgrid_len = forward.shape[1] // 2
    image_len = FACETS * FS
    number = offsets.shape[0]
    xcells = jnp.arange(facet_len, dtype=jnp.int32)
    turn = -TWO_PI * (xcells[None, :] * offsets[:, None] % image_len).astype(jnp.float32) / image_len
    cosine = jnp.cos(turn)[:, None, None, None, :]
    sine_table = jnp.sin(turn)[:, None, None, None, :]
    real_in = facet_blk[..., :facet_len].astype(jnp.float32)[None]
    imag_in = facet_blk[..., facet_len:].astype(jnp.float32)[None]
    shifted = jnp.concatenate([real_in * cosine - imag_in * sine_table, real_in * sine_table + imag_in * cosine], -1).astype(jnp.bfloat16)
    spectra = jnp.dot(shifted.reshape(-1, 2 * facet_len), forward, preferred_element_type=jnp.float32)
    spectra = spectra.reshape(number, facet_count, facet_blk.shape[1], facet_blk.shape[2], 2 * subgrid_len)
    facet_ids = facet_start + jnp.arange(facet_count, dtype=jnp.int32)
    ucells = jnp.arange(subgrid_len, dtype=jnp.int32)
    wraps = facet_ids[None, :, None] * (offsets[:, None, None] + ucells[None, None, :]) % FACETS
    turn_out = -TWO_PI * wraps.astype(jnp.float32) / FACETS
    cosine_out = jnp.cos(turn_out)[:, :, None, None, :]
    sine_out = jnp.sin(turn_out)[:, :, None, None, :]
    real_spec = spectra[..., :subgrid_len]
    imag_spec = spectra[..., subgrid_len:]
    real_sum = lax.optimization_barrier(jnp.sum(real_spec * cosine_out - imag_spec * sine_out, axis=1))
    imag_sum = lax.optimization_barrier(jnp.sum(real_spec * sine_out + imag_spec * cosine_out, axis=1))
    return jnp.concatenate([real_sum, imag_sum], -1) / math.sqrt(image_len)

def to_facets(grid_blk, offsets, facet_start, facet_count, backward):
    number = grid_blk.shape[0]
    subgrid_len = grid_blk.shape[-1] // 2
    facet_len = backward.shape[1] // 2
    image_len = FACETS * FS
    facet_ids = facet_start + jnp.arange(facet_count, dtype=jnp.int32)
    ucells = jnp.arange(subgrid_len, dtype=jnp.int32)
    wraps = facet_ids[None, :, None] * (offsets[:, None, None] + ucells[None, None, :]) % FACETS
    turn_in = TWO_PI * wraps.astype(jnp.float32) / FACETS
    cosine_in = jnp.cos(turn_in)[:, :, None, None, :]
    sine_in = jnp.sin(turn_in)[:, :, None, None, :]
    real_in = grid_blk[..., :subgrid_len].astype(jnp.float32)[:, None]
    imag_in = grid_blk[..., subgrid_len:].astype(jnp.float32)[:, None]
    rotated = jnp.concatenate([real_in * cosine_in - imag_in * sine_in, real_in * sine_in + imag_in * cosine_in], -1).astype(jnp.bfloat16)
    images = jnp.dot(rotated.reshape(-1, 2 * subgrid_len), backward, preferred_element_type=jnp.float32)
    images = images.reshape(number, facet_count, grid_blk.shape[1], grid_blk.shape[2], 2 * facet_len)
    xcells = jnp.arange(facet_len, dtype=jnp.int32)
    turn_x = TWO_PI * (xcells[None, :] * offsets[:, None] % image_len).astype(jnp.float32) / image_len
    cosine_x = jnp.cos(turn_x)[:, None, None, None, :]
    sine_x = jnp.sin(turn_x)[:, None, None, None, :]
    real_img = images[..., :facet_len]
    imag_img = images[..., facet_len:]
    real_sum = lax.optimization_barrier(jnp.sum(real_img * cosine_x - imag_img * sine_x, axis=0))
    imag_sum = lax.optimization_barrier(jnp.sum(real_img * sine_x + imag_img * cosine_x, axis=0))
    return jnp.concatenate([real_sum, imag_sum], -1) / math.sqrt(image_len)

def wave_table(coord):
    columns = jnp.arange(SS, dtype=jnp.int32).astype(jnp.float32)
    turn = TWO_PI * coord[:, 1, :, None] * columns
    return jnp.concatenate([jnp.cos(turn), jnp.sin(turn)], -1).astype(jnp.bfloat16)

def row_phase(coord):
    lines = jnp.arange(ROWS, dtype=jnp.int32).astype(jnp.float32)
    turn = TWO_PI * coord[:, 0, :, None] * lines
    return (jnp.cos(turn), jnp.sin(turn))

def degrid(subs, wave, coord, which):
    sub_count, pol_count, row_count, width_two = subs.shape
    subgrid_len = width_two // 2
    blocks, slots = (coord.shape[0], coord.shape[2])
    real_part = subs[..., :subgrid_len]
    imag_part = subs[..., subgrid_len:]
    first_mat = jnp.concatenate([real_part, -imag_part], -1)
    second_mat = jnp.concatenate([imag_part, real_part], -1)
    stacked = jnp.stack([first_mat, second_mat], 2).reshape(-1, width_two)
    product = jnp.dot(wave.reshape(blocks * slots, width_two), stacked.T, preferred_element_type=jnp.float32)
    product = product.reshape(blocks, slots, sub_count, pol_count, 2, row_count)
    choose = (which[:, None] == jnp.arange(sub_count, dtype=jnp.int32)[None, :]).astype(jnp.float32)
    chosen = lax.optimization_barrier(jnp.sum(product * choose[:, None, :, None, None, None], axis=2))
    cos_rows, sin_rows = row_phase(coord)
    cos_rows = cos_rows[:, :, None, :]
    sin_rows = sin_rows[:, :, None, :]
    real_y = chosen[:, :, :, 0, :]
    imag_y = chosen[:, :, :, 1, :]
    real_pred = lax.optimization_barrier(jnp.sum(cos_rows * real_y - sin_rows * imag_y, -1))
    imag_pred = lax.optimization_barrier(jnp.sum(cos_rows * imag_y + sin_rows * real_y, -1))
    result = jnp.stack([real_pred, imag_pred], -1).transpose(0, 2, 3, 1)
    return result / math.sqrt(ROWS * SS)

def grid(corr, wave, coord, which):
    blocks, pol_count, _, slots = corr.shape
    cos_rows, sin_rows = row_phase(coord)
    cos_rows = cos_rows[:, :, None, :]
    sin_rows = sin_rows[:, :, None, :]
    real_c = corr[:, :, 0, :].transpose(0, 2, 1)[..., None]
    imag_c = corr[:, :, 1, :].transpose(0, 2, 1)[..., None]
    real_z = cos_rows * real_c + sin_rows * imag_c
    imag_z = cos_rows * imag_c - sin_rows * real_c
    stacked = jnp.stack([real_z, imag_z], 3)
    choose = (which[:, None] == jnp.arange(SG_DEV, dtype=jnp.int32)[None, :]).astype(jnp.float32)
    weighted = (stacked[:, :, None] * choose[:, None, :, None, None, None]).astype(jnp.bfloat16)
    summed = jnp.dot(wave.reshape(blocks * slots, 2 * SS).T, weighted.reshape(blocks * slots, -1), preferred_element_type=jnp.float32)
    summed = summed.reshape(2 * SS, SG_DEV, pol_count, 2, ROWS)
    upper = summed[:SS]
    lower = summed[SS:]
    real_q = upper[:, :, :, 0, :] + lower[:, :, :, 1, :]
    imag_q = upper[:, :, :, 1, :] - lower[:, :, :, 0, :]
    result = jnp.concatenate([real_q, imag_q], 0).transpose(1, 2, 3, 0)
    return result / math.sqrt(ROWS * SS)

def reference(facets, subgrid_offset, tile_subgrid, tile_count, vis_coord, stations, jones, observed):
    forward, backward = transform_tables()

    def one_subgrid(offset):
        return to_subgrids(facets, jnp.int32(0), offset.reshape(1), forward)[0]
    subgrids = lax.map(one_subgrid, subgrid_offset).astype(jnp.bfloat16)
    per_worker = TILES // N_WORK

    def one_worker(items):
        subs, coord, which, counts, pairs, seen = items
        wave = wave_table(coord)
        model = degrid(subs, wave, coord, which)
        left = jones_matrix(jones, pairs, 0)
        right = jones_matrix(jones, pairs, 1)
        apparent = apply_jones(left, right, model)
        live = (jnp.arange(TILE, dtype=jnp.int32)[None, :] < counts[:, None]).astype(jnp.float32)[:, None, None, :]
        resid = (seen - apparent) * live
        corrected = adjoint_jones(left, right, resid)
        return (resid, grid(corrected, wave, coord, which))
    items = (subgrids.reshape(N_WORK, SG_DEV, 4, ROWS, 2 * SS), vis_coord.reshape(N_WORK, per_worker, 2, TILE), tile_subgrid.reshape(N_WORK, per_worker), tile_count.reshape(N_WORK, per_worker), stations.reshape(N_WORK, per_worker, 2, TILE), observed.reshape(N_WORK, per_worker, 4, 2, TILE))
    resid, grids = lax.map(one_worker, items)
    residual_vis = resid.reshape(TILES, 4, 2, TILE)
    grids = grids.reshape(SUBGRIDS, 4, ROWS, 2 * SS).astype(jnp.bfloat16)

    def one_facet(index):
        return to_facets(grids, subgrid_offset, index, 1, backward)[0]
    residual_image = lax.map(one_facet, jnp.arange(FACETS, dtype=jnp.int32))
    return (residual_vis, residual_image)
```

```python
import functools
import math

import jax
import jax.numpy as jnp
from jax import lax
from jax.experimental import pallas as pl
from jax.experimental.pallas import tpu as pltpu
from jax.sharding import PartitionSpec as P

SS = 512
STEP = 32
MESH = pl.DeviceIdType.MESH
F32 = jnp.float32
BF16 = jnp.bfloat16
VMEM = pl.BlockSpec(memory_space=pltpu.VMEM)
SMEM = pl.BlockSpec(memory_space=pltpu.SMEM)
LIMIT = 60 * 1024 * 1024


def sincos(turns):
    y = (turns - jnp.floor(turns + 0.5)) * (0.5 * math.pi)
    q = y * y
    s = y * (1.0 + q * (-1 / 6 + q * (1 / 120 + q * (-1 / 5040 + q * (1 / 362880)))))
    c = 1.0 + q * (-1 / 2 + q * (1 / 24 + q * (-1 / 720 + q * (1 / 40320))))
    for _ in range(2):
        s, c = 2.0 * s * c, 1.0 - 2.0 * s * s
    return s, c


def iota(shape, axis):
    return lax.broadcasted_iota(jnp.int32, shape, axis)


def int_turns(product, length):
    return lax.rem(product, length).astype(F32) * (1.0 / length)


def fill_table(cos_ref, sin_ref, image_len):
    rows, cols = cos_ref.shape
    coarse = rows // STEP
    sa, ca = sincos(-int_turns(iota((coarse, cols), 0) * STEP * iota((coarse, cols), 1), image_len))
    sb, cb = sincos(-int_turns(iota((STEP, cols), 0) * iota((STEP, cols), 1), image_len))
    for a in range(coarse):
        s, c = sa[a : a + 1], ca[a : a + 1]
        cos_ref[a * STEP : (a + 1) * STEP, :] = (c * cb - s * sb).astype(BF16)
        sin_ref[a * STEP : (a + 1) * STEP, :] = (s * cb + c * sb).astype(BF16)


def forward_kernel(
    facet_total, per_facet, chunk, off_ref, fac_ref, out_ref, cos_ref, sin_ref, re_ref, im_ref
):
    rows, width_two = fac_ref.shape
    cells = width_two // 2
    count = rows // per_facet
    image_len = facet_total * cells
    step = pl.program_id(0)

    @pl.when(step == 0)
    def _():
        fill_table(cos_ref, sin_ref, image_len)

    start = lax.axis_index("work") * count
    for i in range(chunk):
        offset = off_ref[step * chunk + i]
        s, c = sincos(-int_turns(iota((1, cells), 1) * offset, image_len))
        real = fac_ref[:, :cells].astype(F32)
        imag = fac_ref[:, cells:].astype(F32)
        re_ref[i * rows : (i + 1) * rows, :] = (real * c - imag * s).astype(BF16)
        im_ref[i * rows : (i + 1) * rows, :] = (real * s + imag * c).astype(BF16)
    dot = functools.partial(jnp.dot, preferred_element_type=F32)
    real_spec = dot(re_ref[...], cos_ref[...]) - dot(im_ref[...], sin_ref[...])
    imag_spec = dot(re_ref[...], sin_ref[...]) + dot(im_ref[...], cos_ref[...])
    scale = 1.0 / math.sqrt(image_len)
    for i in range(chunk):
        offset = off_ref[step * chunk + i]
        ids = start + iota((count, SS), 0)
        s, c = sincos(-int_turns(ids * (offset + iota((count, SS), 1)), facet_total))
        real = imag = 0.0
        for f in range(count):
            first = i * rows + f * per_facet
            a = real_spec[first : first + per_facet]
            b = imag_spec[first : first + per_facet]
            real += a * c[f : f + 1] - b * s[f : f + 1]
            imag += a * s[f : f + 1] + b * c[f : f + 1]
        out_ref[i, :, :SS] = (real * scale).astype(BF16)
        out_ref[i, :, SS:] = (imag * scale).astype(BF16)


def chunk_of(number, rows):
    chunk = max(1, min(number, 256 // rows))
    while number % chunk:
        chunk -= 1
    return chunk


def forward(facets, offsets, facet_total):
    count, pols, lines, width_two = facets.shape
    number = offsets.shape[0]
    rows = count * pols * lines
    cells = width_two // 2
    chunk = chunk_of(number, rows)
    return pl.pallas_call(
        functools.partial(forward_kernel, facet_total, pols * lines, chunk),
        out_shape=jax.ShapeDtypeStruct((number, pols * lines, 2 * SS), BF16),
        grid=(number // chunk,),
        in_specs=[SMEM, pl.BlockSpec((rows, width_two), lambda i: (0, 0))],
        out_specs=pl.BlockSpec((chunk, pols * lines, 2 * SS), lambda i: (i, 0, 0)),
        scratch_shapes=[
            pltpu.VMEM((cells, SS), BF16),
            pltpu.VMEM((cells, SS), BF16),
            pltpu.VMEM((chunk * rows, cells), BF16),
            pltpu.VMEM((chunk * rows, cells), BF16),
        ],
        compiler_params=pltpu.CompilerParams(vmem_limit_bytes=LIMIT),
        name="forward",
    )(offsets, facets.reshape(rows, width_two))


def backward_kernel(
    facet_total, count, chunk, off_ref, grid_ref, out_ref, cos_ref, sin_ref, re_ref, im_ref
):
    per_facet = grid_ref.shape[1]
    cells = cos_ref.shape[1]
    rows = count * per_facet
    image_len = facet_total * cells
    step = pl.program_id(0)

    @pl.when(step == 0)
    def _():
        fill_table(cos_ref, sin_ref, image_len)

    start = lax.axis_index("work") * count
    for i in range(chunk):
        offset = off_ref[step * chunk + i]
        ids = start + iota((count, SS), 0)
        s, c = sincos(int_turns(ids * (offset + iota((count, SS), 1)), facet_total))
        real = grid_ref[i, :, :SS].astype(F32)
        imag = grid_ref[i, :, SS:].astype(F32)
        for f in range(count):
            first = i * rows + f * per_facet
            sf, cf = s[f : f + 1], c[f : f + 1]
            re_ref[first : first + per_facet, :] = (real * cf - imag * sf).astype(BF16)
            im_ref[first : first + per_facet, :] = (real * sf + imag * cf).astype(BF16)
    dot = functools.partial(jnp.dot, preferred_element_type=F32)
    real_img = dot(re_ref[...], cos_ref[...]) + dot(im_ref[...], sin_ref[...])
    imag_img = dot(im_ref[...], cos_ref[...]) - dot(re_ref[...], sin_ref[...])
    scale = 1.0 / math.sqrt(image_len)
    real_sum = imag_sum = 0.0
    for i in range(chunk):
        offset = off_ref[step * chunk + i]
        s, c = sincos(int_turns(iota((1, cells), 1) * offset, image_len))
        s, c = s * scale, c * scale
        a = real_img[i * rows : (i + 1) * rows]
        b = imag_img[i * rows : (i + 1) * rows]
        real_sum += a * c - b * s
        imag_sum += a * s + b * c

    @pl.when(step == 0)
    def _():
        out_ref[:, :cells] = real_sum
        out_ref[:, cells:] = imag_sum

    @pl.when(step > 0)
    def _():
        out_ref[:, :cells] += real_sum
        out_ref[:, cells:] += imag_sum


def backward(grids, offsets, facet_total, count, cells):
    number, per_facet, _ = grids.shape
    rows = count * per_facet
    chunk = chunk_of(number, rows)
    return pl.pallas_call(
        functools.partial(backward_kernel, facet_total, count, chunk),
        out_shape=jax.ShapeDtypeStruct((rows, 2 * cells), F32),
        grid=(number // chunk,),
        in_specs=[SMEM, pl.BlockSpec((chunk, per_facet, 2 * SS), lambda i: (i, 0, 0))],
        out_specs=pl.BlockSpec((rows, 2 * cells), lambda i: (0, 0)),
        scratch_shapes=[
            pltpu.VMEM((SS, cells), BF16),
            pltpu.VMEM((SS, cells), BF16),
            pltpu.VMEM((chunk * rows, SS), BF16),
            pltpu.VMEM((chunk * rows, SS), BF16),
        ],
        compiler_params=pltpu.CompilerParams(vmem_limit_bytes=LIMIT),
        name="backward",
    )(offsets, grids)


def cmul(a, b):
    return (a[0] * b[0] - a[1] * b[1], a[0] * b[1] + a[1] * b[0])


def conj(a):
    return (a[0], -a[1])


def cadd(a, b):
    return (a[0] + b[0], a[1] + b[1])


def pick(flag, a, b):
    return (jnp.where(flag, a[0], b[0]), jnp.where(flag, a[1], b[1]))


def visibility_kernel(
    pols, which_ref, count_ref, coord_ref, stat_ref, jones_ref, obs_ref, subs_ref,
    resid_ref, grid_ref, wave_ref, stack_ref, acc_ref, hot_ref, weight_ref,
):
    chips, halves, subs, _, width = subs_ref.shape
    lines = subs_ref.shape[3] // pols
    all_rows = lines * halves
    total = chips * pols
    slots = coord_ref.shape[2]
    step = pl.program_id(0)

    @pl.when(step == 0)
    def _():
        acc_ref[...] = jnp.zeros_like(acc_ref)
        for g in range(subs):
            for p in range(total):
                for h in range(halves):
                    at = (p % pols) * lines
                    both = subs_ref[p // pols, h, g, at : at + lines, :].astype(F32)
                    real, imag = both[:, :SS], both[:, SS:]
                    row = p * all_rows + h * lines
                    low = total * all_rows + row
                    stack_ref[g, row : row + lines, :SS] = real
                    stack_ref[g, row : row + lines, SS:] = -imag
                    stack_ref[g, low : low + lines, :SS] = imag
                    stack_ref[g, low : low + lines, SS:] = real

    coord = coord_ref[0]
    m, l = coord[1:2], coord[0:1]
    coarse = SS // STEP
    sa, ca = sincos(iota((coarse, slots), 0).astype(F32) * STEP * m)
    sb, cb = sincos(iota((STEP, slots), 0).astype(F32) * m)
    for a in range(coarse):
        s, c = sa[a : a + 1], ca[a : a + 1]
        wave_ref[a * STEP : (a + 1) * STEP, :] = (c * cb - s * sb).astype(BF16)
        wave_ref[SS + a * STEP : SS + (a + 1) * STEP, :] = (s * cb + c * sb).astype(BF16)
    sr, cr = sincos(iota((all_rows, slots), 0).astype(F32) * l)

    which = which_ref[step]
    chosen = stack_ref[0]
    for g in range(1, subs):
        chosen = jnp.where(which == g, stack_ref[g], chosen)
    product = jnp.dot(chosen.astype(BF16), wave_ref[...], preferred_element_type=F32)
    scale = 1.0 / math.sqrt(all_rows * SS)
    model = []
    for p in range(total):
        low = (total + p) * all_rows
        y_re = product[p * all_rows : (p + 1) * all_rows]
        y_im = product[low : low + all_rows]
        re = jnp.sum(cr * y_re - sr * y_im, axis=0, keepdims=True) * scale
        im = jnp.sum(cr * y_im + sr * y_re, axis=0, keepdims=True) * scale
        model.append((re, im))

    table = jones_ref[...]
    high = table.astype(BF16)
    rest = table - high.astype(F32)
    middle = rest.astype(BF16)
    low_part = (rest - middle.astype(F32)).astype(BF16)
    parts = jnp.concatenate([high, middle, low_part], 0)
    entries = table.shape[0]
    sides = []
    for side in range(2):
        hot = iota((table.shape[1], slots), 0) == stat_ref[0, side : side + 1, :]
        hot_ref[...] = jnp.where(hot, 1.0, 0.0).astype(BF16)
        got = jnp.dot(parts, hot_ref[...], preferred_element_type=F32)
        got = (got[2 * entries :] + got[entries : 2 * entries]) + got[:entries]
        half = entries // 2
        sides.append([[(got[2 * i + k : 2 * i + k + 1], got[half + 2 * i + k : half + 2 * i + k + 1])
                       for k in range(2)] for i in range(2)])
    left, right = sides

    bright = [[model[2 * i + k] for k in range(2)] for i in range(2)]
    inner = [[cadd(cmul(left[i][0], bright[0][k]), cmul(left[i][1], bright[1][k]))
              for k in range(2)] for i in range(2)]
    outer = [[cadd(cmul(inner[i][0], conj(right[k][0])), cmul(inner[i][1], conj(right[k][1])))
              for k in range(2)] for i in range(2)]
    live = iota((1, slots), 1) < count_ref[step]
    resid = []
    for p in range(total):
        at = (p % pols) * 2
        seen = (obs_ref[p // pols, 0, at : at + 1, :], obs_ref[p // pols, 0, at + 1 : at + 2, :])
        got = outer[p // 2][p % 2]
        resid.append((jnp.where(live, seen[0] - got[0], 0.0), jnp.where(live, seen[1] - got[1], 0.0)))
    mine = lax.axis_index("pol") * pols
    for j in range(pols):
        p = mine + j
        own = resid[0]
        for other in range(1, total):
            own = pick(p == other, resid[other], own)
        resid_ref[0, 2 * j : 2 * j + 1, :] = own[0]
        resid_ref[0, 2 * j + 1 : 2 * j + 2, :] = own[1]
        first, second = p < 2, lax.rem(p, 2) == 0
        l0 = conj(pick(first, left[0][0], left[0][1]))
        l1 = conj(pick(first, left[1][0], left[1][1]))
        r0 = pick(second, right[0][0], right[0][1])
        r1 = pick(second, right[1][0], right[1][1])
        t0 = cadd(cmul(l0, resid[0]), cmul(l1, resid[2]))
        t1 = cadd(cmul(l0, resid[1]), cmul(l1, resid[3]))
        cre, cim = cadd(cmul(t0, r0), cmul(t1, r1))
        row = 2 * j * all_rows
        weight_ref[row : row + all_rows, :] = cr * cre + sr * cim
        weight_ref[row + all_rows : row + 2 * all_rows, :] = cr * cim - sr * cre
    summed = lax.dot_general(
        weight_ref[...].astype(BF16), wave_ref[...], (((1,), (1,)), ((), ())),
        preferred_element_type=F32,
    )
    for g in range(subs):
        acc_ref[g] += jnp.where(which == g, summed, 0.0)

    @pl.when(step == pl.num_programs(0) - 1)
    def _():
        for g in range(subs):
            for j in range(pols):
                row = 2 * j * all_rows
                real_z = acc_ref[g, row : row + all_rows, :]
                imag_z = acc_ref[g, row + all_rows : row + 2 * all_rows, :]
                real = ((real_z[:, :SS] + imag_z[:, SS:]) * scale).astype(BF16)
                imag = ((imag_z[:, :SS] - real_z[:, SS:]) * scale).astype(BF16)
                for h in range(halves):
                    cut = slice(h * lines, (h + 1) * lines)
                    grid_ref[h, g, j * lines : (j + 1) * lines, :SS] = real[cut]
                    grid_ref[h, g, j * lines : (j + 1) * lines, SS:] = imag[cut]


def visibilities(which, counts, coord, stations, jones, seen, subs, pols):
    blocks, _, slots = coord.shape
    chips, halves, sub_count, wide, width = subs.shape
    rows = halves * wide // pols
    total = chips * pols
    return pl.pallas_call(
        functools.partial(visibility_kernel, pols),
        out_shape=(
            jax.ShapeDtypeStruct((blocks, 2 * pols, slots), F32),
            jax.ShapeDtypeStruct((halves, sub_count, wide, width), BF16),
        ),
        grid=(blocks,),
        in_specs=[
            SMEM,
            SMEM,
            pl.BlockSpec((1, 2, slots), lambda i: (i, 0, 0)),
            pl.BlockSpec((1, 2, slots), lambda i: (i, 0, 0)),
            pl.BlockSpec(jones.shape, lambda i: (0, 0)),
            pl.BlockSpec((chips, 1, 2 * pols, slots), lambda i: (0, i, 0, 0)),
            pl.BlockSpec(subs.shape, lambda i: (0, 0, 0, 0, 0)),
        ],
        out_specs=(
            pl.BlockSpec((1, 2 * pols, slots), lambda i: (i, 0, 0)),
            pl.BlockSpec((halves, sub_count, wide, width), lambda i: (0, 0, 0, 0)),
        ),
        scratch_shapes=[
            pltpu.VMEM((2 * SS, slots), BF16),
            pltpu.VMEM((sub_count, 2 * total * rows, width), F32),
            pltpu.VMEM((sub_count, 2 * pols * rows, width), F32),
            pltpu.VMEM((jones.shape[1], slots), BF16),
            pltpu.VMEM((2 * pols * rows, slots), F32),
        ],
        compiler_params=pltpu.CompilerParams(vmem_limit_bytes=LIMIT),
        name="visibilities",
    )(which, counts, coord, stations, jones, seen, subs)


def send(src, dst, send_sem, recv_sem, device):
    copy = pltpu.make_async_remote_copy(
        src_ref=src, dst_ref=dst, send_sem=send_sem, recv_sem=recv_sem,
        device_id=device, device_id_type=MESH,
    )
    copy.start()
    return copy


def meet(devices):
    barrier = pltpu.get_barrier_semaphore()
    for device in devices:
        pl.semaphore_signal(barrier, inc=1, device_id=device, device_id_type=MESH)
    pl.semaphore_wait(barrier, len(devices))


def ahead(name, size, hop):
    return lax.rem(lax.axis_index(name) + hop, size)


def join_kernel(
    work, pol, vis, part_ref, obs_ref, subs_ref, seen_ref,
    land_ref, s_work, r_work, s_out, r_out, s_obs, r_obs,
):
    me, my_pol, my_vis = (lax.axis_index(n) for n in ("work", "pol", "vis"))
    peers = [{"work": ahead("work", work, d)} for d in range(1, work)]
    mates = [
        {"pol": ahead("pol", pol, a), "vis": ahead("vis", vis, b)}
        for a in range(pol) for b in range(vis) if a + b > 0
    ]
    meet(peers + mates)
    copies = [
        send(part_ref.at[ahead("work", work, d)], land_ref.at[d - 1], s_work.at[d - 1],
             r_work.at[d - 1], peers[d - 1])
        for d in range(1, work)
    ]
    seen_copies = [
        send(obs_ref, seen_ref.at[my_pol], s_obs.at[a - 1], r_obs.at[a - 1],
             {"pol": ahead("pol", pol, a)})
        for a in range(1, pol)
    ]
    seen_ref[my_pol] = obs_ref[...]
    total = part_ref[me].astype(F32)
    for d, copy in enumerate(copies):
        copy.wait()
        total += land_ref[d].astype(F32)
    subs_ref[my_pol, my_vis] = total.astype(BF16)
    own = subs_ref.at[my_pol, my_vis]
    spread = [send(own, own, s_out.at[i], r_out.at[i], mate) for i, mate in enumerate(mates)]
    for copy in seen_copies + spread:
        copy.wait()


def join(part, seen, sizes):
    work, pol, vis = sizes
    number, wide, width = part.shape
    mates = pol * vis - 1
    dma = pltpu.SemaphoreType.DMA
    return pl.pallas_call(
        functools.partial(join_kernel, work, pol, vis),
        out_shape=(
            jax.ShapeDtypeStruct((pol, vis, number // work, wide, width), BF16),
            jax.ShapeDtypeStruct((pol,) + seen.shape, F32),
        ),
        in_specs=[VMEM, VMEM],
        out_specs=(VMEM, VMEM),
        scratch_shapes=[
            pltpu.VMEM((work - 1, number // work, wide, width), BF16),
            dma((work - 1,)), dma((work - 1,)), dma((mates,)), dma((mates,)),
            dma((pol - 1,)), dma((pol - 1,)),
        ],
        compiler_params=pltpu.CompilerParams(
            collective_id=0, has_side_effects=True, vmem_limit_bytes=LIMIT
        ),
        name="join",
    )(part.reshape(work, number // work, wide, width), seen)


def spread_kernel(work, vis, part_ref, out_ref, land_ref, s_vis, r_vis, s_work, r_work):
    me, my_vis = lax.axis_index("work"), lax.axis_index("vis")
    peers = [{"work": ahead("work", work, d)} for d in range(1, work)]
    mates = [{"vis": ahead("vis", vis, b)} for b in range(1, vis)]
    meet(peers + mates)
    copies = [
        send(part_ref.at[ahead("vis", vis, b)], land_ref.at[b - 1], s_vis.at[b - 1],
             r_vis.at[b - 1], mates[b - 1])
        for b in range(1, vis)
    ]
    total = part_ref[my_vis].astype(F32)
    for b, copy in enumerate(copies):
        copy.wait()
        total += land_ref[b].astype(F32)
    out_ref[me] = total.astype(BF16)
    own = out_ref.at[me]
    for copy in [send(own, own, s_work.at[d], r_work.at[d], peers[d]) for d in range(work - 1)]:
        copy.wait()


def spread(part, sizes):
    work, pol, vis = sizes
    _, subs, wide, width = part.shape
    dma = pltpu.SemaphoreType.DMA
    return pl.pallas_call(
        functools.partial(spread_kernel, work, vis),
        out_shape=jax.ShapeDtypeStruct((work, subs, wide, width), BF16),
        in_specs=[VMEM],
        out_specs=VMEM,
        scratch_shapes=[
            pltpu.VMEM((vis - 1, subs, wide, width), BF16),
            dma((vis - 1,)), dma((vis - 1,)), dma((work - 1,)), dma((work - 1,)),
        ],
        compiler_params=pltpu.CompilerParams(
            collective_id=1, has_side_effects=True, vmem_limit_bytes=LIMIT
        ),
        name="spread",
    )(part)


def on_device(
    sizes, facets, subgrid_offset, tile_subgrid, tile_count, vis_coord, stations, jones, observed
):
    count, pols, lines, width_two = facets.shape
    blocks, _, _, slots = observed.shape
    facet_total = count * sizes[0]
    part = forward(facets, subgrid_offset, facet_total)
    subs, seen = join(part, observed.reshape(blocks, 2 * pols, slots), sizes)
    resid, grid_part = visibilities(
        tile_subgrid, tile_count, vis_coord, stations, jones, seen, subs, pols
    )
    grids = spread(grid_part, sizes)
    number = subgrid_offset.shape[0]
    image = backward(
        grids.reshape(number, pols * lines, 2 * SS), subgrid_offset, facet_total, count,
        width_two // 2,
    )
    return resid.reshape(observed.shape), image.reshape(facets.shape)


def solution(mesh):
    sizes = tuple(mesh.shape[name] for name in ("work", "pol", "vis"))
    in_specs = (
        P(("groups", "work"), "pol", "vis", None),
        P("groups"),
        P(("groups", "work", "vis")),
        P(("groups", "work", "vis")),
        P(("groups", "work", "vis"), None, None),
        P(("work", "vis"), None, None),
        P(None, "groups"),
        P(("groups", "work", "vis"), "pol", None, None),
    )
    out_specs = (
        P(("groups", "work", "vis"), "pol", None, None),
        P(("groups", "work"), "pol", "vis", None),
    )
    return jax.shard_map(
        functools.partial(on_device, sizes),
        mesh=mesh, in_specs=in_specs, out_specs=out_specs, check_vma=False,
    )
```

```python
import functools
import math

import jax
import jax.numpy as jnp
from jax import lax
from jax.experimental import pallas as pl
from jax.experimental.pallas import tpu as pltpu
from jax.sharding import PartitionSpec as P

SS = 512
STEP = 32
MESH = pl.DeviceIdType.MESH
F32 = jnp.float32
BF16 = jnp.bfloat16
VMEM = pl.BlockSpec(memory_space=pltpu.VMEM)
ANY = pl.BlockSpec(memory_space=pl.ANY)
SMEM = pl.BlockSpec(memory_space=pltpu.SMEM)
LIMIT = 60 * 1024 * 1024


def sincos(turns):
    y = (turns - jnp.floor(turns + 0.5)) * (0.5 * math.pi)
    q = y * y
    s = y * (1.0 + q * (-1 / 6 + q * (1 / 120 + q * (-1 / 5040 + q * (1 / 362880)))))
    c = 1.0 + q * (-1 / 2 + q * (1 / 24 + q * (-1 / 720 + q * (1 / 40320))))
    for _ in range(2):
        s, c = 2.0 * s * c, 1.0 - 2.0 * s * s
    return s, c


def iota(shape, axis):
    return lax.broadcasted_iota(jnp.int32, shape, axis)


def int_turns(product, length):
    return lax.rem(product, length).astype(F32) * (1.0 / length)


def fill_table(cos_ref, sin_ref, image_len):
    rows, cols = cos_ref.shape
    coarse = rows // STEP
    sa, ca = sincos(-int_turns(iota((coarse, cols), 0) * STEP * iota((coarse, cols), 1), image_len))
    sb, cb = sincos(-int_turns(iota((STEP, cols), 0) * iota((STEP, cols), 1), image_len))
    for a in range(coarse):
        s, c = sa[a : a + 1], ca[a : a + 1]
        cos_ref[a * STEP : (a + 1) * STEP, :] = (c * cb - s * sb).astype(BF16)
        sin_ref[a * STEP : (a + 1) * STEP, :] = (s * cb + c * sb).astype(BF16)


def cmul(a, b):
    return (a[0] * b[0] - a[1] * b[1], a[0] * b[1] + a[1] * b[0])


def conj(a):
    return (a[0], -a[1])


def cadd(a, b):
    return (a[0] + b[0], a[1] + b[1])


def pick(flag, a, b):
    return (jnp.where(flag, a[0], b[0]), jnp.where(flag, a[1], b[1]))


def send(src, dst, send_sem, recv_sem, device):
    copy = pltpu.make_async_remote_copy(
        src_ref=src, dst_ref=dst, send_sem=send_sem, recv_sem=recv_sem,
        device_id=device, device_id_type=MESH,
    )
    copy.start()
    return copy


def ahead(name, size, hop):
    return lax.rem(lax.axis_index(name) + hop, size)


def dot(a, b):
    return jnp.dot(a, b, preferred_element_type=F32)


def kernel(
    sizes, off_ref, which_ref, count_ref, fac_hbm, coord_ref, stat_ref, jones_ref, obs_ref,
    resid_ref, image_ref,
    fac_ref, wide_ref, fcos_ref, fsin_ref, bcos_ref, bsin_ref, re_ref, im_ref, bre_ref, bim_ref,
    part_ref, land_ref, subs_ref, seen_ref, wave_ref, phase_ref, gain_ref, hot_ref, stack_ref,
    weight_ref, grid_ref, gpart_ref, gland_ref, grids_ref, image_acc,
    fac_sem, s_work, r_work, s_out, r_out, s_obs, r_obs, s_vis, r_vis, s_grid, r_grid,
):
    work, pol, vis = sizes
    count, pols, lines, width_two = fac_ref.shape
    cells = width_two // 2
    per_facet = pols * lines
    rows = count * per_facet
    subs = part_ref.shape[1]
    facet_total = count * work
    image_len = facet_total * cells
    blocks, _, slots = coord_ref.shape
    all_rows = lines * vis
    total = pols * pol
    me, my_pol, my_vis = (lax.axis_index(n) for n in ("work", "pol", "vis"))
    start = me * count

    def peer(d):
        return {"work": ahead("work", work, d)}

    mates = [
        {"pol": ahead("pol", pol, a), "vis": ahead("vis", vis, b)}
        for a in range(pol) for b in range(vis) if a + b > 0
    ]
    everyone = [peer(d) for d in range(1, work)] + mates
    fetch = pltpu.make_async_copy(fac_hbm, fac_ref, fac_sem)
    fetch.start()
    barrier = pltpu.get_barrier_semaphore()
    for device in everyone:
        pl.semaphore_signal(barrier, inc=1, device_id=device, device_id_type=MESH)
    fill_table(fcos_ref, fsin_ref, image_len)
    fetch.wait()
    for f in range(count):
        for p in range(pols):
            row = f * per_facet + p * lines
            wide_ref[row : row + lines, :] = fac_ref[f, p].astype(F32)
    pl.semaphore_wait(barrier, len(everyone))
    seen_copies = [
        send(obs_ref, seen_ref.at[my_pol], s_obs.at[a - 1], r_obs.at[a - 1],
             {"pol": ahead("pol", pol, a)})
        for a in range(1, pol)
    ]
    seen_ref[my_pol] = obs_ref[...]

    def share(d):
        slot = jnp.maximum(d - 1, 0) if isinstance(d, int) else d - 1
        return pltpu.make_async_remote_copy(
            src_ref=part_ref.at[ahead("work", work, d)], dst_ref=land_ref.at[slot],
            send_sem=s_work.at[slot], recv_sem=r_work.at[slot],
            device_id=peer(d), device_id_type=MESH,
        )

    def forward_step(d):
        owner = ahead("work", work, d)
        for i in range(subs):
            offset = off_ref[owner * subs + i]
            s, c = sincos(-int_turns(iota((1, cells), 1) * offset, image_len))
            real, imag = wide_ref[:, :cells], wide_ref[:, cells:]
            re_ref[i * rows : (i + 1) * rows, :] = (real * c - imag * s).astype(BF16)
            im_ref[i * rows : (i + 1) * rows, :] = (real * s + imag * c).astype(BF16)
        real_spec = dot(re_ref[...], fcos_ref[...]) - dot(im_ref[...], fsin_ref[...])
        imag_spec = dot(re_ref[...], fsin_ref[...]) + dot(im_ref[...], fcos_ref[...])
        scale = 1.0 / math.sqrt(image_len)
        for i in range(subs):
            offset = off_ref[owner * subs + i]
            ids = start + iota((count, SS), 0)
            s, c = sincos(-int_turns(ids * (offset + iota((count, SS), 1)), facet_total))
            real = imag = 0.0
            for f in range(count):
                first = i * rows + f * per_facet
                a = real_spec[first : first + per_facet]
                b = imag_spec[first : first + per_facet]
                real += a * c[f : f + 1] - b * s[f : f + 1]
                imag += a * s[f : f + 1] + b * c[f : f + 1]
            part_ref[owner, i, :, :SS] = (real * scale).astype(BF16)
            part_ref[owner, i, :, SS:] = (imag * scale).astype(BF16)

    def forward_loop(d, carry):
        forward_step(d)

        @pl.when(d < work)
        def _():
            share(d).start()

        return carry

    lax.fori_loop(1, work + 1, forward_loop, 0)

    own_subs = subs_ref.at[my_pol, my_vis]
    spread = [
        pltpu.make_async_remote_copy(
            src_ref=own_subs, dst_ref=own_subs, send_sem=s_out.at[i], recv_sem=r_out.at[i],
            device_id=mate, device_id_type=MESH,
        )
        for i, mate in enumerate(mates)
    ]

    def gather_shares():
        def add(d, carry):
            share(d).wait()
            stack_ref[:, :per_facet, :] += land_ref[d - 1].astype(F32)
            return carry

        stack_ref[:, :per_facet, :] = part_ref[me].astype(F32)
        lax.fori_loop(1, work, add, 0)
        subs_ref[my_pol, my_vis] = stack_ref[:, :per_facet, :].astype(BF16)
        for copy in spread:
            copy.start()

    table = jones_ref[...]
    high = table.astype(BF16)
    rest = table - high.astype(F32)
    middle = rest.astype(BF16)
    low_part = (rest - middle.astype(F32)).astype(BF16)
    parts = jnp.concatenate([high, middle, low_part], 0)
    entries = table.shape[0]
    coarse = SS // STEP

    def prepare(t, carry):
        @pl.when(t == blocks // 2)
        def _():
            gather_shares()

        m, l = coord_ref[t, 1:2, :], coord_ref[t, 0:1, :]
        sa, ca = sincos(iota((coarse, slots), 0).astype(F32) * STEP * m)
        sb, cb = sincos(iota((STEP, slots), 0).astype(F32) * m)
        for a in range(coarse):
            s, c = sa[a : a + 1], ca[a : a + 1]
            wave_ref[t, a * STEP : (a + 1) * STEP, :] = (c * cb - s * sb).astype(BF16)
            wave_ref[t, SS + a * STEP : SS + (a + 1) * STEP, :] = (s * cb + c * sb).astype(BF16)
        sr, cr = sincos(iota((all_rows, slots), 0).astype(F32) * l)
        phase_ref[t, 0] = cr
        phase_ref[t, 1] = sr
        for side in range(2):
            hot = iota((table.shape[1], slots), 0) == stat_ref[t, side : side + 1, :]
            hot_ref[...] = jnp.where(hot, 1.0, 0.0).astype(BF16)
            got = dot(parts, hot_ref[...])
            got = (got[2 * entries :] + got[entries : 2 * entries]) + got[:entries]
            gain_ref[t, side] = got
        return carry

    lax.fori_loop(0, blocks, prepare, 0)

    for copy in seen_copies + spread:
        copy.wait()
    for g in range(subs):
        for p in range(total):
            for h in range(vis):
                at = (p % pols) * lines
                both = subs_ref[p // pols, h, g, at : at + lines, :].astype(F32)
                real, imag = both[:, :SS], both[:, SS:]
                row = p * all_rows + h * lines
                low = total * all_rows + row
                stack_ref[g, row : row + lines, :SS] = real
                stack_ref[g, row : row + lines, SS:] = -imag
                stack_ref[g, low : low + lines, :SS] = imag
                stack_ref[g, low : low + lines, SS:] = real
    grid_ref[...] = jnp.zeros_like(grid_ref)
    scale = 1.0 / math.sqrt(all_rows * SS)
    mine = my_pol * pols

    def degrid(t, carry):
        which = which_ref[t]
        cr, sr = phase_ref[t, 0], phase_ref[t, 1]
        chosen = stack_ref[0]
        for g in range(1, subs):
            chosen = jnp.where(which == g, stack_ref[g], chosen)
        product = dot(chosen.astype(BF16), wave_ref[t])
        model = []
        for p in range(total):
            low = (total + p) * all_rows
            y_re = product[p * all_rows : (p + 1) * all_rows]
            y_im = product[low : low + all_rows]
            re = jnp.sum(cr * y_re - sr * y_im, axis=0, keepdims=True) * scale
            im = jnp.sum(cr * y_im + sr * y_re, axis=0, keepdims=True) * scale
            model.append((re, im))
        half = entries // 2
        left, right = (
            [[(gain_ref[t, side, 2 * i + k : 2 * i + k + 1, :],
               gain_ref[t, side, half + 2 * i + k : half + 2 * i + k + 1, :])
              for k in range(2)] for i in range(2)]
            for side in range(2)
        )
        bright = [[model[2 * i + k] for k in range(2)] for i in range(2)]
        inner = [[cadd(cmul(left[i][0], bright[0][k]), cmul(left[i][1], bright[1][k]))
                  for k in range(2)] for i in range(2)]
        outer = [[cadd(cmul(inner[i][0], conj(right[k][0])), cmul(inner[i][1], conj(right[k][1])))
                  for k in range(2)] for i in range(2)]
        live = iota((1, slots), 1) < count_ref[t]
        resid = []
        for p in range(total):
            got = outer[p // 2][p % 2]
            resid.append(tuple(
                jnp.where(live, seen_ref[p // pols, t, p % pols, n : n + 1, :] - got[n], 0.0)
                for n in range(2)
            ))
        for j in range(pols):
            p = mine + j
            own = resid[0]
            for other in range(1, total):
                own = pick(p == other, resid[other], own)
            resid_ref[t, j, 0:1, :] = own[0]
            resid_ref[t, j, 1:2, :] = own[1]
            first, second = p < 2, lax.rem(p, 2) == 0
            l0 = conj(pick(first, left[0][0], left[0][1]))
            l1 = conj(pick(first, left[1][0], left[1][1]))
            r0 = pick(second, right[0][0], right[0][1])
            r1 = pick(second, right[1][0], right[1][1])
            t0 = cadd(cmul(l0, resid[0]), cmul(l1, resid[2]))
            t1 = cadd(cmul(l0, resid[1]), cmul(l1, resid[3]))
            cre, cim = cadd(cmul(t0, r0), cmul(t1, r1))
            row = 2 * j * all_rows
            weight_ref[row : row + all_rows, :] = cr * cre + sr * cim
            weight_ref[row + all_rows : row + 2 * all_rows, :] = cr * cim - sr * cre
        summed = lax.dot_general(
            weight_ref[...].astype(BF16), wave_ref[t], (((1,), (1,)), ((), ())),
            preferred_element_type=F32,
        )
        for g in range(subs):
            grid_ref[g] += jnp.where(which == g, summed, 0.0)
        return carry

    lax.fori_loop(0, blocks, degrid, 0)

    for g in range(subs):
        for j in range(pols):
            row = 2 * j * all_rows
            real_z = grid_ref[g, row : row + all_rows, :]
            imag_z = grid_ref[g, row + all_rows : row + 2 * all_rows, :]
            real = ((real_z[:, :SS] + imag_z[:, SS:]) * scale).astype(BF16)
            imag = ((imag_z[:, :SS] - real_z[:, SS:]) * scale).astype(BF16)
            for h in range(vis):
                cut = slice(h * lines, (h + 1) * lines)
                gpart_ref[h, g, j * lines : (j + 1) * lines, :SS] = real[cut]
                gpart_ref[h, g, j * lines : (j + 1) * lines, SS:] = imag[cut]
    halves = [
        send(gpart_ref.at[ahead("vis", vis, b)], gland_ref.at[b - 1], s_vis.at[b - 1],
             r_vis.at[b - 1], {"vis": ahead("vis", vis, b)})
        for b in range(1, vis)
    ]
    fill_table(bcos_ref, bsin_ref, image_len)
    both = gpart_ref[my_vis].astype(F32)
    for b, copy in enumerate(halves):
        copy.wait()
        both += gland_ref[b].astype(F32)
    grids_ref[me] = both.astype(BF16)

    def grid_copy(d):
        own = grids_ref.at[me]
        return pltpu.make_async_remote_copy(
            src_ref=own, dst_ref=own, send_sem=s_grid.at[d - 1], recv_sem=r_grid.at[d - 1],
            device_id=peer(d), device_id_type=MESH,
        )

    for d in range(1, work):
        grid_copy(d).start()
    image_acc[...] = jnp.zeros_like(image_acc)

    def backward_step(d, carry):
        @pl.when(d > 0)
        def _():
            grid_copy(d).wait()

        owner = ahead("work", work, work - d)
        for i in range(subs):
            offset = off_ref[owner * subs + i]
            ids = start + iota((count, SS), 0)
            s, c = sincos(int_turns(ids * (offset + iota((count, SS), 1)), facet_total))
            real = grids_ref[owner, i, :, :SS].astype(F32)
            imag = grids_ref[owner, i, :, SS:].astype(F32)
            for f in range(count):
                first = i * rows + f * per_facet
                sf, cf = s[f : f + 1], c[f : f + 1]
                bre_ref[first : first + per_facet, :] = (real * cf - imag * sf).astype(BF16)
                bim_ref[first : first + per_facet, :] = (real * sf + imag * cf).astype(BF16)
        real_img = dot(bre_ref[...], bcos_ref[...]) + dot(bim_ref[...], bsin_ref[...])
        imag_img = dot(bim_ref[...], bcos_ref[...]) - dot(bre_ref[...], bsin_ref[...])
        unit = 1.0 / math.sqrt(image_len)
        real_sum = imag_sum = 0.0
        for i in range(subs):
            offset = off_ref[owner * subs + i]
            s, c = sincos(int_turns(iota((1, cells), 1) * offset, image_len))
            s, c = s * unit, c * unit
            a = real_img[i * rows : (i + 1) * rows]
            b = imag_img[i * rows : (i + 1) * rows]
            real_sum += a * c - b * s
            imag_sum += a * s + b * c
        image_acc[:, :cells] += real_sum
        image_acc[:, cells:] += imag_sum
        return carry

    lax.fori_loop(0, work, backward_step, 0)
    for f in range(count):
        for p in range(pols):
            row = f * per_facet + p * lines
            image_ref[f, p] = image_acc[row : row + lines, :]


def on_device(
    sizes, facets, subgrid_offset, tile_subgrid, tile_count, vis_coord, stations, jones, observed
):
    work, pol, vis = sizes
    count, pols, lines, width_two = facets.shape
    blocks, _, _, slots = observed.shape
    subs = subgrid_offset.shape[0] // work
    cells, wide = width_two // 2, pols * lines
    rows = count * wide
    all_rows, total = lines * vis, pols * pol
    block = (subs, wide, 2 * SS)
    dma = pltpu.SemaphoreType.DMA
    mates = pol * vis - 1
    return pl.pallas_call(
        functools.partial(kernel, sizes),
        out_shape=(
            jax.ShapeDtypeStruct(observed.shape, F32),
            jax.ShapeDtypeStruct(facets.shape, F32),
        ),
        in_specs=[SMEM, SMEM, SMEM, ANY, VMEM, VMEM, VMEM, VMEM],
        out_specs=(VMEM, VMEM),
        scratch_shapes=[
            pltpu.VMEM(facets.shape, BF16),
            pltpu.VMEM((rows, width_two), F32),
            pltpu.VMEM((cells, SS), BF16),
            pltpu.VMEM((cells, SS), BF16),
            pltpu.VMEM((SS, cells), BF16),
            pltpu.VMEM((SS, cells), BF16),
            pltpu.VMEM((subs * rows, cells), BF16),
            pltpu.VMEM((subs * rows, cells), BF16),
            pltpu.VMEM((subs * rows, SS), BF16),
            pltpu.VMEM((subs * rows, SS), BF16),
            pltpu.VMEM((work,) + block, BF16),
            pltpu.VMEM((work - 1,) + block, BF16),
            pltpu.VMEM((pol, vis) + block, BF16),
            pltpu.VMEM((pol,) + observed.shape, F32),
            pltpu.VMEM((blocks, 2 * SS, slots), BF16),
            pltpu.VMEM((blocks, 2, all_rows, slots), F32),
            pltpu.VMEM((blocks, 2) + (jones.shape[0], slots), F32),
            pltpu.VMEM((jones.shape[1], slots), BF16),
            pltpu.VMEM((subs, 2 * total * all_rows, 2 * SS), F32),
            pltpu.VMEM((2 * pols * all_rows, slots), F32),
            pltpu.VMEM((subs, 2 * pols * all_rows, 2 * SS), F32),
            pltpu.VMEM((vis,) + block, BF16),
            pltpu.VMEM((vis - 1,) + block, BF16),
            pltpu.VMEM((work,) + block, BF16),
            pltpu.VMEM((rows, width_two), F32),
            dma,
            dma((work - 1,)), dma((work - 1,)), dma((mates,)), dma((mates,)),
            dma((pol - 1,)), dma((pol - 1,)), dma((vis - 1,)), dma((vis - 1,)),
            dma((work - 1,)), dma((work - 1,)),
        ],
        compiler_params=pltpu.CompilerParams(
            collective_id=0, has_side_effects=True, vmem_limit_bytes=LIMIT
        ),
        name="cycle",
    )(subgrid_offset, tile_subgrid, tile_count, facets, vis_coord, stations, jones, observed)


def solution(mesh):
    sizes = tuple(mesh.shape[name] for name in ("work", "pol", "vis"))
    in_specs = (
        P(("groups", "work"), "pol", "vis", None),
        P("groups"),
        P(("groups", "work", "vis")),
        P(("groups", "work", "vis")),
        P(("groups", "work", "vis"), None, None),
        P(("work", "vis"), None, None),
        P(None, "groups"),
        P(("groups", "work", "vis"), "pol", None, None),
    )
    out_specs = (
        P(("groups", "work", "vis"), "pol", None, None),
        P(("groups", "work"), "pol", "vis", None),
    )
    return jax.shard_map(
        functools.partial(on_device, sizes),
        mesh=mesh, in_specs=in_specs, out_specs=out_specs, check_vma=False,
    )
```

```python
import functools
import math

import jax
import jax.numpy as jnp
from jax import lax
from jax.experimental import pallas as pl
from jax.experimental.pallas import tpu as pltpu
from jax.sharding import PartitionSpec as P

SS = 512
STEP = 32
MESH = pl.DeviceIdType.MESH
F32 = jnp.float32
BF16 = jnp.bfloat16
VMEM = pl.BlockSpec(memory_space=pltpu.VMEM)
SMEM = pl.BlockSpec(memory_space=pltpu.SMEM)
LIMIT = 30 * 1024 * 1024


def sincos(turns):
    y = (turns - jnp.floor(turns + 0.5)) * (0.5 * math.pi)
    q = y * y
    s = y * (1.0 + q * (-1 / 6 + q * (1 / 120 + q * (-1 / 5040 + q * (1 / 362880)))))
    c = 1.0 + q * (-1 / 2 + q * (1 / 24 + q * (-1 / 720 + q * (1 / 40320))))
    for _ in range(2):
        s, c = 2.0 * s * c, 1.0 - 2.0 * s * s
    return s, c


def iota(shape, axis):
    return lax.broadcasted_iota(jnp.int32, shape, axis)


def int_turns(product, length):
    return lax.rem(product, length).astype(F32) * (1.0 / length)


def fill_table(cos_ref, sin_ref, image_len):
    rows, cols = cos_ref.shape
    coarse = rows // STEP
    sa, ca = sincos(-int_turns(iota((coarse, cols), 0) * STEP * iota((coarse, cols), 1), image_len))
    sb, cb = sincos(-int_turns(iota((STEP, cols), 0) * iota((STEP, cols), 1), image_len))
    for a in range(coarse):
        s, c = sa[a : a + 1], ca[a : a + 1]
        cos_ref[a * STEP : (a + 1) * STEP, :] = (c * cb - s * sb).astype(BF16)
        sin_ref[a * STEP : (a + 1) * STEP, :] = (s * cb + c * sb).astype(BF16)


def cmul(a, b):
    return (a[0] * b[0] - a[1] * b[1], a[0] * b[1] + a[1] * b[0])


def conj(a):
    return (a[0], -a[1])


def cadd(a, b):
    return (a[0] + b[0], a[1] + b[1])


def pick(flag, a, b):
    return (jnp.where(flag, a[0], b[0]), jnp.where(flag, a[1], b[1]))


def send(src, dst, send_sem, recv_sem, device):
    copy = pltpu.make_async_remote_copy(
        src_ref=src, dst_ref=dst, send_sem=send_sem, recv_sem=recv_sem,
        device_id=device, device_id_type=MESH,
    )
    copy.start()
    return copy


def ahead(name, size, hop):
    return lax.rem(lax.axis_index(name) + hop, size)


def dot(a, b):
    return jnp.dot(a, b, preferred_element_type=F32)


def kernel(
    sizes, off_ref, which_ref, count_ref, fac_ref, coord_ref, stat_ref, jones_ref, obs_ref,
    resid_ref, image_ref,
    wide_ref, fcos_ref, fsin_ref, bcos_ref, bsin_ref, re_ref, im_ref, bre_ref, bim_ref,
    part_ref, land_ref, subs_ref, seen_ref, wave_ref, phase_ref, gain_ref, hot_ref, stack_ref,
    weight_ref, grid_ref, gpart_ref, gland_ref, grids_ref, image_acc,
    s_work, r_work, s_out, r_out, s_obs, r_obs, s_vis, r_vis, s_grid, r_grid,
):
    work, pol, vis = sizes
    count, pols, lines, width_two = fac_ref.shape
    cells = width_two // 2
    per_facet = pols * lines
    rows = count * per_facet
    subs = part_ref.shape[1]
    facet_total = count * work
    image_len = facet_total * cells
    blocks, _, slots = coord_ref.shape
    all_rows = lines * vis
    total = pols * pol
    me, my_pol, my_vis = (lax.axis_index(n) for n in ("work", "pol", "vis"))
    start = me * count

    def peer(d):
        return {"work": ahead("work", work, d)}

    mates = [
        {"pol": ahead("pol", pol, a), "vis": ahead("vis", vis, b)}
        for a in range(pol) for b in range(vis) if a + b > 0
    ]
    everyone = [peer(d) for d in range(1, work)] + mates
    barrier = pltpu.get_barrier_semaphore()
    for device in everyone:
        pl.semaphore_signal(barrier, inc=1, device_id=device, device_id_type=MESH)
    fill_table(fcos_ref, fsin_ref, image_len)
    for f in range(count):
        for p in range(pols):
            row = f * per_facet + p * lines
            wide_ref[row : row + lines, :] = fac_ref[f, p].astype(F32)
    pl.semaphore_wait(barrier, len(everyone))
    seen_copies = [
        send(obs_ref, seen_ref.at[my_pol], s_obs.at[a - 1], r_obs.at[a - 1],
             {"pol": ahead("pol", pol, a)})
        for a in range(1, pol)
    ]
    seen_ref[my_pol] = obs_ref[...]

    def share(d):
        slot = jnp.maximum(d - 1, 0) if isinstance(d, int) else d - 1
        return pltpu.make_async_remote_copy(
            src_ref=part_ref.at[ahead("work", work, d)], dst_ref=land_ref.at[slot],
            send_sem=s_work.at[slot], recv_sem=r_work.at[slot],
            device_id=peer(d), device_id_type=MESH,
        )

    def forward_step(d):
        owner = ahead("work", work, d)
        for i in range(subs):
            offset = off_ref[owner * subs + i]
            s, c = sincos(-int_turns(iota((1, cells), 1) * offset, image_len))
            real, imag = wide_ref[:, :cells], wide_ref[:, cells:]
            re_ref[i * rows : (i + 1) * rows, :] = (real * c - imag * s).astype(BF16)
            im_ref[i * rows : (i + 1) * rows, :] = (real * s + imag * c).astype(BF16)
        real_spec = dot(re_ref[...], fcos_ref[...]) - dot(im_ref[...], fsin_ref[...])
        imag_spec = dot(re_ref[...], fsin_ref[...]) + dot(im_ref[...], fcos_ref[...])
        scale = 1.0 / math.sqrt(image_len)
        for i in range(subs):
            offset = off_ref[owner * subs + i]
            ids = start + iota((count, SS), 0)
            s, c = sincos(-int_turns(ids * (offset + iota((count, SS), 1)), facet_total))
            real = imag = 0.0
            for f in range(count):
                first = i * rows + f * per_facet
                a = real_spec[first : first + per_facet]
                b = imag_spec[first : first + per_facet]
                real += a * c[f : f + 1] - b * s[f : f + 1]
                imag += a * s[f : f + 1] + b * c[f : f + 1]
            part_ref[owner, i, :, :SS] = (real * scale).astype(BF16)
            part_ref[owner, i, :, SS:] = (imag * scale).astype(BF16)

    def forward_loop(d, carry):
        forward_step(d)

        @pl.when(d < work)
        def _():
            share(d).start()

        return carry

    lax.fori_loop(1, work + 1, forward_loop, 0)

    own_subs = subs_ref.at[my_pol, my_vis]
    spread = [
        pltpu.make_async_remote_copy(
            src_ref=own_subs, dst_ref=own_subs, send_sem=s_out.at[i], recv_sem=r_out.at[i],
            device_id=mate, device_id_type=MESH,
        )
        for i, mate in enumerate(mates)
    ]

    def gather_shares():
        def add(d, carry):
            share(d).wait()
            stack_ref[:, :per_facet, :] += land_ref[d - 1].astype(F32)
            return carry

        stack_ref[:, :per_facet, :] = part_ref[me].astype(F32)
        lax.fori_loop(1, work, add, 0)
        subs_ref[my_pol, my_vis] = stack_ref[:, :per_facet, :].astype(BF16)
        for copy in spread:
            copy.start()

    table = jones_ref[...]
    high = table.astype(BF16)
    rest = table - high.astype(F32)
    middle = rest.astype(BF16)
    low_part = (rest - middle.astype(F32)).astype(BF16)
    parts = jnp.concatenate([high, middle, low_part], 0)
    entries = table.shape[0]
    coarse = SS // STEP

    def prepare(t, carry):
        @pl.when(t == blocks // 2)
        def _():
            gather_shares()

        m, l = coord_ref[t, 1:2, :], coord_ref[t, 0:1, :]
        sa, ca = (x.astype(BF16) for x in sincos(iota((coarse, slots), 0).astype(F32) * STEP * m))
        sb, cb = (x.astype(BF16) for x in sincos(iota((STEP, slots), 0).astype(F32) * m))
        for a in range(coarse):
            s, c = sa[a : a + 1], ca[a : a + 1]
            wave_ref[t, a * STEP : (a + 1) * STEP, :] = c * cb - s * sb
            wave_ref[t, SS + a * STEP : SS + (a + 1) * STEP, :] = s * cb + c * sb
        sr, cr = sincos(iota((all_rows, slots), 0).astype(F32) * l)
        phase_ref[t, 0] = cr
        phase_ref[t, 1] = sr
        for side in range(2):
            station = stat_ref[t, side : side + 1, :]
            near = jnp.where(iota((STEP, slots), 0) == station % STEP, 1.0, 0.0).astype(BF16)
            groups = table.shape[1] // STEP
            far = jnp.where(iota((groups, slots), 0) == station // STEP, 1.0, 0.0).astype(BF16)
            for a in range(groups):
                hot_ref[a * STEP : (a + 1) * STEP, :] = far[a : a + 1] * near
            got = dot(parts, hot_ref[...])
            got = (got[2 * entries :] + got[entries : 2 * entries]) + got[:entries]
            gain_ref[t, side] = got
        return carry

    lax.fori_loop(0, blocks, prepare, 0)

    for copy in seen_copies + spread:
        copy.wait()
    for g in range(subs):
        for p in range(total):
            for h in range(vis):
                at = (p % pols) * lines
                both = subs_ref[p // pols, h, g, at : at + lines, :].astype(F32)
                real, imag = both[:, :SS], both[:, SS:]
                row = p * all_rows + h * lines
                low = total * all_rows + row
                stack_ref[g, row : row + lines, :SS] = real
                stack_ref[g, row : row + lines, SS:] = -imag
                stack_ref[g, low : low + lines, :SS] = imag
                stack_ref[g, low : low + lines, SS:] = real
    grid_ref[...] = jnp.zeros_like(grid_ref)
    scale = 1.0 / math.sqrt(all_rows * SS)
    mine = my_pol * pols

    def degrid(t, carry):
        which = which_ref[t]
        cr, sr = phase_ref[t, 0], phase_ref[t, 1]
        chosen = stack_ref[0]
        for g in range(1, subs):
            chosen = jnp.where(which == g, stack_ref[g], chosen)
        product = dot(chosen.astype(BF16), wave_ref[t])
        model = []
        for p in range(total):
            low = (total + p) * all_rows
            y_re = product[p * all_rows : (p + 1) * all_rows]
            y_im = product[low : low + all_rows]
            re = jnp.sum(cr * y_re - sr * y_im, axis=0, keepdims=True) * scale
            im = jnp.sum(cr * y_im + sr * y_re, axis=0, keepdims=True) * scale
            model.append((re, im))
        half = entries // 2
        left, right = (
            [[(gain_ref[t, side, 2 * i + k : 2 * i + k + 1, :],
               gain_ref[t, side, half + 2 * i + k : half + 2 * i + k + 1, :])
              for k in range(2)] for i in range(2)]
            for side in range(2)
        )
        bright = [[model[2 * i + k] for k in range(2)] for i in range(2)]
        inner = [[cadd(cmul(left[i][0], bright[0][k]), cmul(left[i][1], bright[1][k]))
                  for k in range(2)] for i in range(2)]
        outer = [[cadd(cmul(inner[i][0], conj(right[k][0])), cmul(inner[i][1], conj(right[k][1])))
                  for k in range(2)] for i in range(2)]
        live = iota((1, slots), 1) < count_ref[t]
        resid = []
        for p in range(total):
            got = outer[p // 2][p % 2]
            resid.append(tuple(
                jnp.where(live, seen_ref[p // pols, t, p % pols, n : n + 1, :] - got[n], 0.0)
                for n in range(2)
            ))
        for j in range(pols):
            p = mine + j
            own = resid[0]
            for other in range(1, total):
                own = pick(p == other, resid[other], own)
            resid_ref[t, j, 0:1, :] = own[0]
            resid_ref[t, j, 1:2, :] = own[1]
            first, second = p < 2, lax.rem(p, 2) == 0
            l0 = conj(pick(first, left[0][0], left[0][1]))
            l1 = conj(pick(first, left[1][0], left[1][1]))
            r0 = pick(second, right[0][0], right[0][1])
            r1 = pick(second, right[1][0], right[1][1])
            t0 = cadd(cmul(l0, resid[0]), cmul(l1, resid[2]))
            t1 = cadd(cmul(l0, resid[1]), cmul(l1, resid[3]))
            cre, cim = cadd(cmul(t0, r0), cmul(t1, r1))
            row = 2 * j * all_rows
            weight_ref[row : row + all_rows, :] = cr * cre + sr * cim
            weight_ref[row + all_rows : row + 2 * all_rows, :] = cr * cim - sr * cre
        summed = lax.dot_general(
            weight_ref[...].astype(BF16), wave_ref[t], (((1,), (1,)), ((), ())),
            preferred_element_type=F32,
        )
        for g in range(subs):
            grid_ref[g] += jnp.where(which == g, summed, 0.0)
        return carry

    lax.fori_loop(0, blocks, degrid, 0)

    for g in range(subs):
        for j in range(pols):
            row = 2 * j * all_rows
            real_z = grid_ref[g, row : row + all_rows, :]
            imag_z = grid_ref[g, row + all_rows : row + 2 * all_rows, :]
            real = ((real_z[:, :SS] + imag_z[:, SS:]) * scale).astype(BF16)
            imag = ((imag_z[:, :SS] - real_z[:, SS:]) * scale).astype(BF16)
            for h in range(vis):
                cut = slice(h * lines, (h + 1) * lines)
                gpart_ref[h, g, j * lines : (j + 1) * lines, :SS] = real[cut]
                gpart_ref[h, g, j * lines : (j + 1) * lines, SS:] = imag[cut]
    halves = [
        send(gpart_ref.at[ahead("vis", vis, b)], gland_ref.at[b - 1], s_vis.at[b - 1],
             r_vis.at[b - 1], {"vis": ahead("vis", vis, b)})
        for b in range(1, vis)
    ]
    fill_table(bcos_ref, bsin_ref, image_len)
    both = gpart_ref[my_vis].astype(F32)
    for b, copy in enumerate(halves):
        copy.wait()
        both += gland_ref[b].astype(F32)
    grids_ref[me] = both.astype(BF16)

    def grid_copy(d):
        own = grids_ref.at[me]
        return pltpu.make_async_remote_copy(
            src_ref=own, dst_ref=own, send_sem=s_grid.at[d - 1], recv_sem=r_grid.at[d - 1],
            device_id=peer(d), device_id_type=MESH,
        )

    for d in range(1, work):
        grid_copy(d).start()
    image_acc[...] = jnp.zeros_like(image_acc)

    def backward_step(d, carry):
        @pl.when(d > 0)
        def _():
            grid_copy(d).wait()

        owner = ahead("work", work, work - d)
        for i in range(subs):
            offset = off_ref[owner * subs + i]
            ids = start + iota((count, SS), 0)
            s, c = sincos(int_turns(ids * (offset + iota((count, SS), 1)), facet_total))
            real = grids_ref[owner, i, :, :SS].astype(F32)
            imag = grids_ref[owner, i, :, SS:].astype(F32)
            for f in range(count):
                first = i * rows + f * per_facet
                sf, cf = s[f : f + 1], c[f : f + 1]
                bre_ref[first : first + per_facet, :] = (real * cf - imag * sf).astype(BF16)
                bim_ref[first : first + per_facet, :] = (real * sf + imag * cf).astype(BF16)
        real_img = dot(bre_ref[...], bcos_ref[...]) + dot(bim_ref[...], bsin_ref[...])
        imag_img = dot(bim_ref[...], bcos_ref[...]) - dot(bre_ref[...], bsin_ref[...])
        unit = 1.0 / math.sqrt(image_len)
        real_sum = imag_sum = 0.0
        for i in range(subs):
            offset = off_ref[owner * subs + i]
            s, c = sincos(int_turns(iota((1, cells), 1) * offset, image_len))
            s, c = s * unit, c * unit
            a = real_img[i * rows : (i + 1) * rows]
            b = imag_img[i * rows : (i + 1) * rows]
            real_sum += a * c - b * s
            imag_sum += a * s + b * c
        image_acc[:, :cells] += real_sum
        image_acc[:, cells:] += imag_sum
        return carry

    lax.fori_loop(0, work, backward_step, 0)
    for f in range(count):
        for p in range(pols):
            row = f * per_facet + p * lines
            image_ref[f, p] = image_acc[row : row + lines, :]


def on_device(
    sizes, facets, subgrid_offset, tile_subgrid, tile_count, vis_coord, stations, jones, observed
):
    work, pol, vis = sizes
    count, pols, lines, width_two = facets.shape
    blocks, _, _, slots = observed.shape
    subs = subgrid_offset.shape[0] // work
    cells, wide = width_two // 2, pols * lines
    rows = count * wide
    all_rows, total = lines * vis, pols * pol
    block = (subs, wide, 2 * SS)
    dma = pltpu.SemaphoreType.DMA
    mates = pol * vis - 1
    return pl.pallas_call(
        functools.partial(kernel, sizes),
        out_shape=(
            jax.ShapeDtypeStruct(observed.shape, F32),
            jax.ShapeDtypeStruct(facets.shape, F32),
        ),
        in_specs=[SMEM, SMEM, SMEM, VMEM, VMEM, VMEM, VMEM, VMEM],
        out_specs=(VMEM, VMEM),
        scratch_shapes=[
            pltpu.VMEM((rows, width_two), F32),
            pltpu.VMEM((cells, SS), BF16),
            pltpu.VMEM((cells, SS), BF16),
            pltpu.VMEM((SS, cells), BF16),
            pltpu.VMEM((SS, cells), BF16),
            pltpu.VMEM((subs * rows, cells), BF16),
            pltpu.VMEM((subs * rows, cells), BF16),
            pltpu.VMEM((subs * rows, SS), BF16),
            pltpu.VMEM((subs * rows, SS), BF16),
            pltpu.VMEM((work,) + block, BF16),
            pltpu.VMEM((work - 1,) + block, BF16),
            pltpu.VMEM((pol, vis) + block, BF16),
            pltpu.VMEM((pol,) + observed.shape, F32),
            pltpu.VMEM((blocks, 2 * SS, slots), BF16),
            pltpu.VMEM((blocks, 2, all_rows, slots), F32),
            pltpu.VMEM((blocks, 2) + (jones.shape[0], slots), F32),
            pltpu.VMEM((jones.shape[1], slots), BF16),
            pltpu.VMEM((subs, 2 * total * all_rows, 2 * SS), F32),
            pltpu.VMEM((2 * pols * all_rows, slots), F32),
            pltpu.VMEM((subs, 2 * pols * all_rows, 2 * SS), F32),
            pltpu.VMEM((vis,) + block, BF16),
            pltpu.VMEM((vis - 1,) + block, BF16),
            pltpu.VMEM((work,) + block, BF16),
            pltpu.VMEM((rows, width_two), F32),
            dma((work - 1,)), dma((work - 1,)), dma((mates,)), dma((mates,)),
            dma((pol - 1,)), dma((pol - 1,)), dma((vis - 1,)), dma((vis - 1,)),
            dma((work - 1,)), dma((work - 1,)),
        ],
        compiler_params=pltpu.CompilerParams(
            collective_id=0, has_side_effects=True, vmem_limit_bytes=LIMIT
        ),
        name="cycle",
    )(subgrid_offset, tile_subgrid, tile_count, facets, vis_coord, stations, jones, observed)


def solution(mesh):
    sizes = tuple(mesh.shape[name] for name in ("work", "pol", "vis"))
    in_specs = (
        P(("groups", "work"), "pol", "vis", None),
        P("groups"),
        P(("groups", "work", "vis")),
        P(("groups", "work", "vis")),
        P(("groups", "work", "vis"), None, None),
        P(("work", "vis"), None, None),
        P(None, "groups"),
        P(("groups", "work", "vis"), "pol", None, None),
    )
    out_specs = (
        P(("groups", "work", "vis"), "pol", None, None),
        P(("groups", "work"), "pol", "vis", None),
    )
    return jax.shard_map(
        functools.partial(on_device, sizes),
        mesh=mesh, in_specs=in_specs, out_specs=out_specs, check_vma=False,
    )
```

```python
import functools
import math

import jax
import jax.numpy as jnp
from jax import lax
from jax.experimental import pallas as pl
from jax.experimental.pallas import tpu as pltpu
from jax.sharding import PartitionSpec as P

SS = 512
STEP = 32
MESH = pl.DeviceIdType.MESH
F32 = jnp.float32
BF16 = jnp.bfloat16
VMEM = pl.BlockSpec(memory_space=pltpu.VMEM)
HBM = pl.BlockSpec(memory_space=pltpu.HBM)
SMEM = pl.BlockSpec(memory_space=pltpu.SMEM)
LIMIT = 30 * 1024 * 1024


def sincos(turns):
    y = (turns - jnp.floor(turns + 0.5)) * (0.5 * math.pi)
    q = y * y
    s = y * (1.0 + q * (-1 / 6 + q * (1 / 120 + q * (-1 / 5040 + q * (1 / 362880)))))
    c = 1.0 + q * (-1 / 2 + q * (1 / 24 + q * (-1 / 720 + q * (1 / 40320))))
    for _ in range(2):
        s, c = 2.0 * s * c, 1.0 - 2.0 * s * s
    return s, c


def iota(shape, axis):
    return lax.broadcasted_iota(jnp.int32, shape, axis)


def int_turns(product, length):
    return lax.rem(product, length).astype(F32) * (1.0 / length)


def fill_table(cos_ref, sin_ref, image_len):
    rows, cols = cos_ref.shape
    coarse = rows // STEP
    sa, ca = sincos(-int_turns(iota((coarse, cols), 0) * STEP * iota((coarse, cols), 1), image_len))
    sb, cb = sincos(-int_turns(iota((STEP, cols), 0) * iota((STEP, cols), 1), image_len))
    for a in range(coarse):
        s, c = sa[a : a + 1], ca[a : a + 1]
        cos_ref[a * STEP : (a + 1) * STEP, :] = (c * cb - s * sb).astype(BF16)
        sin_ref[a * STEP : (a + 1) * STEP, :] = (s * cb + c * sb).astype(BF16)


def cmul(a, b):
    return (a[0] * b[0] - a[1] * b[1], a[0] * b[1] + a[1] * b[0])


def conj(a):
    return (a[0], -a[1])


def cadd(a, b):
    return (a[0] + b[0], a[1] + b[1])


def pick(flag, a, b):
    return (jnp.where(flag, a[0], b[0]), jnp.where(flag, a[1], b[1]))


def send(src, dst, send_sem, recv_sem, device):
    copy = pltpu.make_async_remote_copy(
        src_ref=src, dst_ref=dst, send_sem=send_sem, recv_sem=recv_sem,
        device_id=device, device_id_type=MESH,
    )
    copy.start()
    return copy


def ahead(name, size, hop):
    return lax.rem(lax.axis_index(name) + hop, size)


def dot(a, b):
    return jnp.dot(a, b, preferred_element_type=F32)


def kernel(
    sizes, off_ref, which_ref, count_ref, fac_hbm, coord_ref, stat_ref, jones_ref, obs_ref,
    resid_ref, image_ref,
    fac_ref, wide_ref, fcos_ref, fsin_ref, bcos_ref, bsin_ref, re_ref, im_ref, bre_ref, bim_ref,
    part_ref, land_ref, subs_ref, seen_ref, wave_ref, phase_ref, gain_ref, hot_ref, stack_ref,
    weight_ref, grid_ref, gpart_ref, gland_ref, grids_ref, image_acc,
    fac_sem, s_work, r_work, s_out, r_out, s_obs, r_obs, s_vis, r_vis, s_grid, r_grid,
):
    work, pol, vis = sizes
    count, pols, lines, width_two = fac_ref.shape
    cells = width_two // 2
    per_facet = pols * lines
    rows = count * per_facet
    subs = part_ref.shape[1]
    facet_total = count * work
    image_len = facet_total * cells
    blocks, _, slots = coord_ref.shape
    all_rows = lines * vis
    total = pols * pol
    me, my_pol, my_vis = (lax.axis_index(n) for n in ("work", "pol", "vis"))
    start = me * count

    def peer(d):
        return {"work": ahead("work", work, d)}

    mates = [
        {"pol": ahead("pol", pol, a), "vis": ahead("vis", vis, b)}
        for a in range(pol) for b in range(vis) if a + b > 0
    ]
    everyone = [peer(d) for d in range(1, work)] + mates
    fetch = pltpu.make_async_copy(fac_hbm, fac_ref, fac_sem)
    fetch.start()
    barrier = pltpu.get_barrier_semaphore()
    for device in everyone:
        pl.semaphore_signal(barrier, inc=1, device_id=device, device_id_type=MESH)
    fill_table(fcos_ref, fsin_ref, image_len)
    fetch.wait()
    for f in range(count):
        for p in range(pols):
            row = f * per_facet + p * lines
            wide_ref[row : row + lines, :] = fac_ref[f, p].astype(F32)
    pl.semaphore_wait(barrier, len(everyone))
    seen_copies = [
        send(obs_ref, seen_ref.at[my_pol], s_obs.at[a - 1], r_obs.at[a - 1],
             {"pol": ahead("pol", pol, a)})
        for a in range(1, pol)
    ]
    seen_ref[my_pol] = obs_ref[...]

    def share(d):
        slot = jnp.maximum(d - 1, 0) if isinstance(d, int) else d - 1
        return pltpu.make_async_remote_copy(
            src_ref=part_ref.at[ahead("work", work, d)], dst_ref=land_ref.at[slot],
            send_sem=s_work.at[slot], recv_sem=r_work.at[slot],
            device_id=peer(d), device_id_type=MESH,
        )

    def forward_step(d):
        owner = ahead("work", work, d)
        for i in range(subs):
            offset = off_ref[owner * subs + i]
            s, c = sincos(-int_turns(iota((1, cells), 1) * offset, image_len))
            real, imag = wide_ref[:, :cells], wide_ref[:, cells:]
            re_ref[i * rows : (i + 1) * rows, :] = (real * c - imag * s).astype(BF16)
            im_ref[i * rows : (i + 1) * rows, :] = (real * s + imag * c).astype(BF16)
        real_spec = dot(re_ref[...], fcos_ref[...]) - dot(im_ref[...], fsin_ref[...])
        imag_spec = dot(re_ref[...], fsin_ref[...]) + dot(im_ref[...], fcos_ref[...])
        scale = 1.0 / math.sqrt(image_len)
        for i in range(subs):
            offset = off_ref[owner * subs + i]
            ids = start + iota((count, SS), 0)
            s, c = sincos(-int_turns(ids * (offset + iota((count, SS), 1)), facet_total))
            real = imag = 0.0
            for f in range(count):
                first = i * rows + f * per_facet
                a = real_spec[first : first + per_facet]
                b = imag_spec[first : first + per_facet]
                real += a * c[f : f + 1] - b * s[f : f + 1]
                imag += a * s[f : f + 1] + b * c[f : f + 1]
            part_ref[owner, i, :, :SS] = (real * scale).astype(BF16)
            part_ref[owner, i, :, SS:] = (imag * scale).astype(BF16)

    def forward_loop(d, carry):
        forward_step(d)

        @pl.when(d < work)
        def _():
            share(d).start()

        return carry

    lax.fori_loop(1, work + 1, forward_loop, 0)

    own_subs = subs_ref.at[my_pol, my_vis]
    spread = [
        pltpu.make_async_remote_copy(
            src_ref=own_subs, dst_ref=own_subs, send_sem=s_out.at[i], recv_sem=r_out.at[i],
            device_id=mate, device_id_type=MESH,
        )
        for i, mate in enumerate(mates)
    ]

    def gather_shares():
        def add(d, carry):
            share(d).wait()
            stack_ref[:, :per_facet, :] += land_ref[d - 1].astype(F32)
            return carry

        stack_ref[:, :per_facet, :] = part_ref[me].astype(F32)
        lax.fori_loop(1, work, add, 0)
        subs_ref[my_pol, my_vis] = stack_ref[:, :per_facet, :].astype(BF16)
        for copy in spread:
            copy.start()

    table = jones_ref[...]
    high = table.astype(BF16)
    rest = table - high.astype(F32)
    middle = rest.astype(BF16)
    low_part = (rest - middle.astype(F32)).astype(BF16)
    parts = jnp.concatenate([high, middle, low_part], 0)
    entries = table.shape[0]
    coarse = SS // STEP

    def prepare(t, carry):
        @pl.when(t == blocks // 2)
        def _():
            gather_shares()

        m, l = coord_ref[t, 1:2, :], coord_ref[t, 0:1, :]
        sa, ca = (x.astype(BF16) for x in sincos(iota((coarse, slots), 0).astype(F32) * STEP * m))
        sb, cb = (x.astype(BF16) for x in sincos(iota((STEP, slots), 0).astype(F32) * m))
        for a in range(coarse):
            s, c = sa[a : a + 1], ca[a : a + 1]
            wave_ref[t, a * STEP : (a + 1) * STEP, :] = c * cb - s * sb
            wave_ref[t, SS + a * STEP : SS + (a + 1) * STEP, :] = s * cb + c * sb
        sr, cr = sincos(iota((all_rows, slots), 0).astype(F32) * l)
        phase_ref[t, 0] = cr
        phase_ref[t, 1] = sr
        for side in range(2):
            station = stat_ref[t, side : side + 1, :]
            near = jnp.where(iota((STEP, slots), 0) == station % STEP, 1.0, 0.0).astype(BF16)
            groups = table.shape[1] // STEP
            far = jnp.where(iota((groups, slots), 0) == station // STEP, 1.0, 0.0).astype(BF16)
            for a in range(groups):
                hot_ref[a * STEP : (a + 1) * STEP, :] = far[a : a + 1] * near
            got = dot(parts, hot_ref[...])
            got = (got[2 * entries :] + got[entries : 2 * entries]) + got[:entries]
            gain_ref[t, side] = got
        return carry

    lax.fori_loop(0, blocks, prepare, 0)

    for copy in seen_copies + spread:
        copy.wait()
    for g in range(subs):
        for p in range(total):
            for h in range(vis):
                at = (p % pols) * lines
                both = subs_ref[p // pols, h, g, at : at + lines, :].astype(F32)
                real, imag = both[:, :SS], both[:, SS:]
                row = p * all_rows + h * lines
                low = total * all_rows + row
                stack_ref[g, row : row + lines, :SS] = real
                stack_ref[g, row : row + lines, SS:] = -imag
                stack_ref[g, low : low + lines, :SS] = imag
                stack_ref[g, low : low + lines, SS:] = real
    grid_ref[...] = jnp.zeros_like(grid_ref)
    scale = 1.0 / math.sqrt(all_rows * SS)
    mine = my_pol * pols

    def degrid(t, carry):
        which = which_ref[t]
        cr, sr = phase_ref[t, 0], phase_ref[t, 1]
        chosen = stack_ref[0]
        for g in range(1, subs):
            chosen = jnp.where(which == g, stack_ref[g], chosen)
        product = dot(chosen.astype(BF16), wave_ref[t])
        model = []
        for p in range(total):
            low = (total + p) * all_rows
            y_re = product[p * all_rows : (p + 1) * all_rows]
            y_im = product[low : low + all_rows]
            re = jnp.sum(cr * y_re - sr * y_im, axis=0, keepdims=True) * scale
            im = jnp.sum(cr * y_im + sr * y_re, axis=0, keepdims=True) * scale
            model.append((re, im))
        half = entries // 2
        left, right = (
            [[(gain_ref[t, side, 2 * i + k : 2 * i + k + 1, :],
               gain_ref[t, side, half + 2 * i + k : half + 2 * i + k + 1, :])
              for k in range(2)] for i in range(2)]
            for side in range(2)
        )
        bright = [[model[2 * i + k] for k in range(2)] for i in range(2)]
        inner = [[cadd(cmul(left[i][0], bright[0][k]), cmul(left[i][1], bright[1][k]))
                  for k in range(2)] for i in range(2)]
        outer = [[cadd(cmul(inner[i][0], conj(right[k][0])), cmul(inner[i][1], conj(right[k][1])))
                  for k in range(2)] for i in range(2)]
        live = iota((1, slots), 1) < count_ref[t]
        resid = []
        for p in range(total):
            got = outer[p // 2][p % 2]
            resid.append(tuple(
                jnp.where(live, seen_ref[p // pols, t, p % pols, n : n + 1, :] - got[n], 0.0)
                for n in range(2)
            ))
        for j in range(pols):
            p = mine + j
            own = resid[0]
            for other in range(1, total):
                own = pick(p == other, resid[other], own)
            resid_ref[t, j, 0:1, :] = own[0]
            resid_ref[t, j, 1:2, :] = own[1]
            first, second = p < 2, lax.rem(p, 2) == 0
            l0 = conj(pick(first, left[0][0], left[0][1]))
            l1 = conj(pick(first, left[1][0], left[1][1]))
            r0 = pick(second, right[0][0], right[0][1])
            r1 = pick(second, right[1][0], right[1][1])
            t0 = cadd(cmul(l0, resid[0]), cmul(l1, resid[2]))
            t1 = cadd(cmul(l0, resid[1]), cmul(l1, resid[3]))
            cre, cim = cadd(cmul(t0, r0), cmul(t1, r1))
            row = 2 * j * all_rows
            weight_ref[row : row + all_rows, :] = cr * cre + sr * cim
            weight_ref[row + all_rows : row + 2 * all_rows, :] = cr * cim - sr * cre
        summed = lax.dot_general(
            weight_ref[...].astype(BF16), wave_ref[t], (((1,), (1,)), ((), ())),
            preferred_element_type=F32,
        )
        for g in range(subs):
            grid_ref[g] += jnp.where(which == g, summed, 0.0)
        return carry

    lax.fori_loop(0, blocks, degrid, 0)

    for g in range(subs):
        for j in range(pols):
            row = 2 * j * all_rows
            real_z = grid_ref[g, row : row + all_rows, :]
            imag_z = grid_ref[g, row + all_rows : row + 2 * all_rows, :]
            real = ((real_z[:, :SS] + imag_z[:, SS:]) * scale).astype(BF16)
            imag = ((imag_z[:, :SS] - real_z[:, SS:]) * scale).astype(BF16)
            for h in range(vis):
                cut = slice(h * lines, (h + 1) * lines)
                gpart_ref[h, g, j * lines : (j + 1) * lines, :SS] = real[cut]
                gpart_ref[h, g, j * lines : (j + 1) * lines, SS:] = imag[cut]
    halves = [
        send(gpart_ref.at[ahead("vis", vis, b)], gland_ref.at[b - 1], s_vis.at[b - 1],
             r_vis.at[b - 1], {"vis": ahead("vis", vis, b)})
        for b in range(1, vis)
    ]
    fill_table(bcos_ref, bsin_ref, image_len)
    both = gpart_ref[my_vis].astype(F32)
    for b, copy in enumerate(halves):
        copy.wait()
        both += gland_ref[b].astype(F32)
    grids_ref[me] = both.astype(BF16)

    def grid_copy(d):
        own = grids_ref.at[me]
        return pltpu.make_async_remote_copy(
            src_ref=own, dst_ref=own, send_sem=s_grid.at[d - 1], recv_sem=r_grid.at[d - 1],
            device_id=peer(d), device_id_type=MESH,
        )

    for d in range(1, work):
        grid_copy(d).start()
    image_acc[...] = jnp.zeros_like(image_acc)

    def backward_step(d, carry):
        @pl.when(d > 0)
        def _():
            grid_copy(d).wait()

        owner = ahead("work", work, work - d)
        for i in range(subs):
            offset = off_ref[owner * subs + i]
            ids = start + iota((count, SS), 0)
            s, c = sincos(int_turns(ids * (offset + iota((count, SS), 1)), facet_total))
            real = grids_ref[owner, i, :, :SS].astype(F32)
            imag = grids_ref[owner, i, :, SS:].astype(F32)
            for f in range(count):
                first = i * rows + f * per_facet
                sf, cf = s[f : f + 1], c[f : f + 1]
                bre_ref[first : first + per_facet, :] = (real * cf - imag * sf).astype(BF16)
                bim_ref[first : first + per_facet, :] = (real * sf + imag * cf).astype(BF16)
        real_img = dot(bre_ref[...], bcos_ref[...]) + dot(bim_ref[...], bsin_ref[...])
        imag_img = dot(bim_ref[...], bcos_ref[...]) - dot(bre_ref[...], bsin_ref[...])
        unit = 1.0 / math.sqrt(image_len)
        real_sum = imag_sum = 0.0
        for i in range(subs):
            offset = off_ref[owner * subs + i]
            s, c = sincos(int_turns(iota((1, cells), 1) * offset, image_len))
            s, c = s * unit, c * unit
            a = real_img[i * rows : (i + 1) * rows]
            b = imag_img[i * rows : (i + 1) * rows]
            real_sum += a * c - b * s
            imag_sum += a * s + b * c
        image_acc[:, :cells] += real_sum
        image_acc[:, cells:] += imag_sum
        return carry

    lax.fori_loop(0, work, backward_step, 0)
    for f in range(count):
        for p in range(pols):
            row = f * per_facet + p * lines
            image_ref[f, p] = image_acc[row : row + lines, :]


def on_device(
    sizes, facets, subgrid_offset, tile_subgrid, tile_count, vis_coord, stations, jones, observed
):
    work, pol, vis = sizes
    count, pols, lines, width_two = facets.shape
    blocks, _, _, slots = observed.shape
    subs = subgrid_offset.shape[0] // work
    cells, wide = width_two // 2, pols * lines
    rows = count * wide
    all_rows, total = lines * vis, pols * pol
    block = (subs, wide, 2 * SS)
    dma = pltpu.SemaphoreType.DMA
    mates = pol * vis - 1
    return pl.pallas_call(
        functools.partial(kernel, sizes),
        out_shape=(
            jax.ShapeDtypeStruct(observed.shape, F32),
            jax.ShapeDtypeStruct(facets.shape, F32),
        ),
        in_specs=[SMEM, SMEM, SMEM, HBM, VMEM, VMEM, VMEM, VMEM],
        out_specs=(VMEM, VMEM),
        scratch_shapes=[
            pltpu.VMEM(facets.shape, BF16),
            pltpu.VMEM((rows, width_two), F32),
            pltpu.VMEM((cells, SS), BF16),
            pltpu.VMEM((cells, SS), BF16),
            pltpu.VMEM((SS, cells), BF16),
            pltpu.VMEM((SS, cells), BF16),
            pltpu.VMEM((subs * rows, cells), BF16),
            pltpu.VMEM((subs * rows, cells), BF16),
            pltpu.VMEM((subs * rows, SS), BF16),
            pltpu.VMEM((subs * rows, SS), BF16),
            pltpu.VMEM((work,) + block, BF16),
            pltpu.VMEM((work - 1,) + block, BF16),
            pltpu.VMEM((pol, vis) + block, BF16),
            pltpu.VMEM((pol,) + observed.shape, F32),
            pltpu.VMEM((blocks, 2 * SS, slots), BF16),
            pltpu.VMEM((blocks, 2, all_rows, slots), F32),
            pltpu.VMEM((blocks, 2) + (jones.shape[0], slots), F32),
            pltpu.VMEM((jones.shape[1], slots), BF16),
            pltpu.VMEM((subs, 2 * total * all_rows, 2 * SS), F32),
            pltpu.VMEM((2 * pols * all_rows, slots), F32),
            pltpu.VMEM((subs, 2 * pols * all_rows, 2 * SS), F32),
            pltpu.VMEM((vis,) + block, BF16),
            pltpu.VMEM((vis - 1,) + block, BF16),
            pltpu.VMEM((work,) + block, BF16),
            pltpu.VMEM((rows, width_two), F32),
            dma,
            dma((work - 1,)), dma((work - 1,)), dma((mates,)), dma((mates,)),
            dma((pol - 1,)), dma((pol - 1,)), dma((vis - 1,)), dma((vis - 1,)),
            dma((work - 1,)), dma((work - 1,)),
        ],
        compiler_params=pltpu.CompilerParams(
            collective_id=0, has_side_effects=True, vmem_limit_bytes=LIMIT
        ),
        name="cycle",
    )(*(
        pltpu.with_memory_space_constraint(x, pltpu.HBM)
        for x in (subgrid_offset, tile_subgrid, tile_count, facets, vis_coord, stations, jones,
                  observed)
    ))


def solution(mesh):
    sizes = tuple(mesh.shape[name] for name in ("work", "pol", "vis"))
    in_specs = (
        P(("groups", "work"), "pol", "vis", None),
        P("groups"),
        P(("groups", "work", "vis")),
        P(("groups", "work", "vis")),
        P(("groups", "work", "vis"), None, None),
        P(("work", "vis"), None, None),
        P(None, "groups"),
        P(("groups", "work", "vis"), "pol", None, None),
    )
    out_specs = (
        P(("groups", "work", "vis"), "pol", None, None),
        P(("groups", "work"), "pol", "vis", None),
    )
    return jax.shard_map(
        functools.partial(on_device, sizes),
        mesh=mesh, in_specs=in_specs, out_specs=out_specs, check_vma=False,
    )
```
